512 devices in a mesh: row: 16 (over x, y), col: 32 (over z, core).
Axes of the slice: x: 4, y: 4, z: 16, core: 2. Of those that a mesh axis runs over, the one named last changes fastest.
Arguments:
- inputs: bfloat16 [768, 6144], P('col', 'row'), may hold values from -6 to 6
- weight: bfloat16 [6144, 24576], P('row', 'col'), may hold values from -0.078125 to 0.078125
- cotangent: bfloat16 [768, 24576], P('row', 'col'), may hold values from -6 to 6
Outputs:
- input_grad: bfloat16 [768, 6144], P('col', 'row')
- weight_grad: float32 [6144, 24576], P('row', 'col')
The draws below stay inside these ranges and needn't reach their ends.
All inputs are finite; a program needn't handle non-finite values.
Results may differ from the reference program's by a relative error of at most 0.0049.
Values may be sent and summed in bfloat16 or wider, within the bound.
A program may use at most 64 MiB of HBM per device.

```python
import jax
import jax.numpy as jnp
from jax import lax

D = 6144
FF = 24576
TOKENS = 768


def strengthened(array, key, source, target, shards_of, factor):
    def block_of(dim):
        return (jnp.arange(array.shape[dim]) // (array.shape[dim] // shards_of)).reshape((-1,) + (1,) * (array.ndim - 1 - dim))

    one_side = jax.random.permutation(key, shards_of)[block_of(target)]
    second = (block_of(target) + shards_of // 2) % shards_of
    return jnp.where((block_of(source) == one_side) | (block_of(source) == second), factor * array, array)


def steps_of(rng, shape, cuts, low, high):
    def one(axis_at, parts):
        draws = jax.random.uniform(jax.random.fold_in(jax.random.fold_in(rng, 6), axis_at), (parts,), jnp.float32, low / len(cuts), high / len(cuts))
        return jnp.repeat(jnp.exp(draws), shape[axis_at] // parts).reshape((-1,) + (1,) * (len(shape) - axis_at - 1))

    level = one(*cuts[0])
    for cut in cuts[1:]:
        level = level * one(*cut)
    return level


def bell_draw(stream_key, shape, scale, reach, shards=(), dtype=jnp.bfloat16):
    result = jax.random.normal(stream_key, shape, jnp.float32) * scale
    if len(shards) > 0:
        result = steps_of(stream_key, shape, shards, -0.22, 0.18) * result
    return jnp.clip(result, min=-reach, max=reach).astype(dtype)


def bell_draw_with(stream_key, shape, spread, reach, shards, heavy, held_as=jnp.bfloat16):
    entries = spread * jax.random.normal(stream_key, shape, jnp.float32)
    if shards:
        entries = entries * steps_of(stream_key, shape, shards, -0.22, 0.18)
    return jnp.clip(strengthened(entries, jax.random.fold_in(stream_key, 3), *heavy), -reach, reach).astype(held_as)


def setup_inputs(seed: int = 0) -> dict:
    streams_of = jax.random.split(jax.random.key(seed), 4)
    return {
        "inputs": bell_draw_with(streams_of[0], (TOKENS, D), 1.0, 6.0, ((0, 32), (1, 16)), (1, 0, 32, 2.75)),
        "weight": bell_draw(streams_of[1], (D, FF), D ** -0.5, 0.078125, ((0, 16), (1, 32))),
        "cotangent": bell_draw_with(streams_of[2], (TOKENS, FF), 1.0, 6.0, ((0, 16), (1, 32)), (1, 0, 32, 2.75)),
    }


def gelu_slope(preact):
    return 0.5 * (1.0 + jax.scipy.special.erf(preact * 0.7071067811865476)) + preact * jnp.exp(-0.5 * preact * preact) * 0.3989422804014327


def reference(inputs, weight, cotangent):
    preact = jnp.dot(inputs, weight, preferred_element_type=jnp.float32)
    grad_hidden = (cotangent.astype(jnp.float32) * gelu_slope(preact)).astype(jnp.bfloat16)
    input_grad = lax.dot_general(grad_hidden, weight, (((1,), (1,)), ((), ())), preferred_element_type=jnp.float32).astype(jnp.bfloat16)
    weight_grad = lax.dot_general(inputs, grad_hidden, (((0,), (0,)), ((), ())), preferred_element_type=jnp.float32)
    return input_grad, weight_grad
```

```python
import functools
import math

import jax
import jax.numpy as jnp
from jax import lax
from jax.experimental import pallas as pl
from jax.experimental.pallas import tpu as pltpu
from jax.sharding import PartitionSpec as P

MESH = pl.DeviceIdType.MESH
F32 = jnp.float32
BF16 = jnp.bfloat16


def gelu_slope(preact):
    return (
        0.5 * (1.0 + lax.erf(preact * 0.7071067811865476))
        + preact * jnp.exp(-0.5 * preact * preact) * 0.3989422804014327
    )


def kernel(
    rows,
    cols,
    x_ref,
    w_ref,
    ct_ref,
    ig_ref,
    wg_ref,
    gat,
    part,
    pin,
    gh,
    full,
    give,
    take,
    pair,
    landed,
    acc,
    zs,
    zr,
    fs,
    fr,
    ps,
    pr,
    gs,
    gr,
    es,
    er,
    qs,
    qr,
):
    ny = math.isqrt(rows)
    nx = rows // ny
    nz = cols // 2
    r = lax.axis_index("row")
    c = lax.axis_index("col")
    z = c // 2
    core = c % 2
    other = 2 * z + 1 - core
    x0 = r // ny
    y0 = r % ny
    share = x_ref.shape[0]
    width = x_ref.shape[1]
    hidden = w_ref.shape[1]
    toks = ct_ref.shape[0]

    def z_peer(d):
        return 2 * ((z + d) % nz) + core

    def near(k):
        half = (k + 1) // 2
        odd = k % 2
        return odd * half + (1 - odd) * (nz - half)

    def row_at(k):
        return ((x0 + k // ny) % nx) * ny + (y0 + k % ny) % ny

    def row_from(k):
        return ((x0 + nx - k // ny) % nx) * ny + (y0 + ny - k % ny) % ny

    def to(src, dst, send, recv, row, col):
        return pltpu.make_async_remote_copy(
            src_ref=src,
            dst_ref=dst,
            send_sem=send,
            recv_sem=recv,
            device_id=(row, col),
            device_id_type=MESH,
        )

    barrier = pltpu.get_barrier_semaphore()

    @pl.loop(1, nz)
    def _(k):
        pl.semaphore_signal(barrier, inc=1, device_id=(r, z_peer(near(k))), device_id_type=MESH)

    @pl.loop(1, rows)
    def _(k):
        pl.semaphore_signal(barrier, inc=1, device_id=(row_at(k), c), device_id_type=MESH)

    pl.semaphore_signal(barrier, inc=1, device_id=(r, other), device_id_type=MESH)
    pl.semaphore_wait(barrier, nz - 1 + rows - 1 + 1)

    @pl.loop(1, nz)
    def _(k):
        d = near(k)
        to(x_ref, gat.at[c], zs.at[d], zr.at[d], r, z_peer(d)).start()

    to(x_ref, gat.at[c], fs.at[0], fr.at[0], r, other).start()
    gat[pl.ds(c, 1)] = x_ref[...].reshape(1, share, width)

    @pl.loop(1, nz)
    def _(k):
        d = near(k)
        from_col = 2 * ((z + nz - d) % nz) + core
        to(x_ref, gat.at[from_col], zs.at[d], zr.at[d], r, c).wait_recv()
        to(gat.at[from_col], gat.at[from_col], fs.at[d], fr.at[d], r, other).start()

    @pl.loop(0, nz)
    def _(k):
        from_col = 2 * ((z + nz - k) % nz) + 1 - core
        to(x_ref, gat.at[from_col], fs.at[k], fr.at[k], r, other).wait_recv()

    for g in range(nx):
        xg = (x0 + g) % nx
        lhs = gat[pl.ds(2 * ny * xg, 2 * ny)].reshape(ny * toks, width)
        block = jnp.dot(lhs, w_ref[...], preferred_element_type=F32)
        if g == 0:
            full[...] = block.reshape(ny, toks, hidden)
            acc[...] = full[pl.ds(y0, 1)].reshape(toks, hidden)
        part[pl.ds(ny * xg, ny)] = block.astype(BF16).reshape(ny, toks, hidden)

        @pl.loop(1 if g == 0 else 0, ny)
        def _(j):
            k = g * ny + j
            peer = row_at(k)
            to(part.at[peer], pin.at[k], ps.at[k], pr.at[k], peer, c).start()

    @pl.loop(1, rows)
    def _(k):
        to(part.at[k], pin.at[k], ps.at[k], pr.at[k], r, other).wait_recv()
        acc[...] += pin[pl.ds(k, 1)].reshape(toks, hidden).astype(F32)

    gh[pl.ds(r, 1)] = (
        (ct_ref[...].astype(F32) * gelu_slope(acc[...])).astype(BF16).reshape(1, toks, hidden)
    )

    @pl.loop(1, rows)
    def _(k):
        to(gh.at[r], gh.at[r], gs.at[k], gr.at[k], row_at(k), c).start()

    for g in range(nx):
        xg = (x0 + nx - g) % nx

        @pl.loop(1 if g == 0 else 0, ny)
        def _(j):
            k = g * ny + j
            to(gh.at[r], gh.at[row_from(k)], gs.at[k], gr.at[k], r, other).wait_recv()

        lhs = gh[pl.ds(ny * xg, ny)].reshape(ny * toks, hidden)
        block = lax.dot_general(
            lhs, w_ref[...], (((1,), (1,)), ((), ())), preferred_element_type=F32
        )
        pair[pl.ds(2 * ny * xg, 2 * ny)] = block.reshape(2 * ny, share, width)
        for j in range(ny):
            at = ny * xg + j
            give[pl.ds(at, 1)] = pair[pl.ds(2 * at + 1 - core, 1)].astype(BF16)
        groups = pl.ds(ny * xg, ny)
        to(give.at[groups], take.at[groups], es.at[g], er.at[g], r, other).start()

    for g in range(nx):
        xg = (x0 + nx - g) % nx
        groups = pl.ds(ny * xg, ny)
        to(give.at[groups], take.at[groups], es.at[g], er.at[g], r, other).wait()

    for k in range(nz):
        at = (z + k) % nz
        mine = pair[pl.ds(2 * at + core, 1)] + take[pl.ds(at, 1)].astype(F32)
        if k == 0:
            pair[pl.ds(c, 1)] = mine
        else:
            give[pl.ds(at, 1)] = mine.astype(BF16)
            to(give.at[at], landed.at[k], qs.at[k], qr.at[k], r, z_peer(k)).start()

    wg_ref[...] = lax.dot_general(
        gat[...].reshape(rows * toks, width),
        gh[...].reshape(rows * toks, hidden),
        (((0,), (0,)), ((), ())),
        preferred_element_type=F32,
    )

    total = pair[pl.ds(c, 1)].reshape(share, width)
    for k in range(1, nz):
        to(give.at[k], landed.at[k], qs.at[k], qr.at[k], r, other).wait_recv()
        total = total + landed[k].astype(F32)
    ig_ref[...] = total.astype(BF16)

    to(x_ref, gat.at[c], fs.at[0], fr.at[0], r, other).wait_send()

    @pl.loop(1, nz)
    def _(k):
        to(x_ref, gat.at[c], zs.at[k], zr.at[k], r, other).wait_send()
        to(x_ref, gat.at[c], fs.at[k], fr.at[k], r, other).wait_send()
        to(give.at[0], landed.at[k], qs.at[k], qr.at[k], r, other).wait_send()

    @pl.loop(1, rows)
    def _(k):
        to(part.at[k], pin.at[k], ps.at[k], pr.at[k], r, other).wait_send()
        to(gh.at[r], gh.at[r], gs.at[k], gr.at[k], r, other).wait_send()


def shards(rows, cols, inputs, weight, cotangent):
    share, width = inputs.shape
    hidden = weight.shape[1]
    toks = cotangent.shape[0]
    nz = cols // 2
    ny = math.isqrt(rows)
    dma = pltpu.SemaphoreType.DMA
    return pl.pallas_call(
        functools.partial(kernel, rows, cols),
        out_shape=(
            jax.ShapeDtypeStruct((share, width), BF16),
            jax.ShapeDtypeStruct((width, hidden), F32),
        ),
        in_specs=[pl.BlockSpec(memory_space=pltpu.VMEM)] * 3,
        out_specs=(pl.BlockSpec(memory_space=pltpu.VMEM),) * 2,
        scratch_shapes=[
            pltpu.VMEM((cols, share, width), BF16),
            pltpu.VMEM((rows, toks, hidden), BF16),
            pltpu.VMEM((rows, toks, hidden), BF16),
            pltpu.VMEM((rows, toks, hidden), BF16),
            pltpu.VMEM((ny, toks, hidden), F32),
            pltpu.VMEM((nz, share, width), BF16),
            pltpu.VMEM((nz, share, width), BF16),
            pltpu.VMEM((cols, share, width), F32),
            pltpu.VMEM((nz, share, width), BF16),
            pltpu.VMEM((toks, hidden), F32),
            dma((nz,)),
            dma((nz,)),
            dma((nz,)),
            dma((nz,)),
            dma((rows,)),
            dma((rows,)),
            dma((rows,)),
            dma((rows,)),
            dma((ny,)),
            dma((ny,)),
            dma((nz,)),
            dma((nz,)),
        ],
        compiler_params=pltpu.CompilerParams(
            collective_id=0, has_side_effects=True, vmem_limit_bytes=56 * 1024 * 1024
        ),
    )(inputs, weight, cotangent)


def solution(mesh):
    rows, cols = mesh.shape["row"], mesh.shape["col"]
    placed = (P("col", "row"), P("row", "col"), P("row", "col"))
    return jax.shard_map(
        functools.partial(shards, rows, cols),
        mesh=mesh,
        in_specs=placed,
        out_specs=(P("col", "row"), P("row", "col")),
        check_vma=False,
    )
```

```python
import functools
import math

import jax
import jax.numpy as jnp
from jax import lax
from jax.experimental import pallas as pl
from jax.experimental.pallas import tpu as pltpu
from jax.sharding import PartitionSpec as P

MESH = pl.DeviceIdType.MESH
F32 = jnp.float32
BF16 = jnp.bfloat16


def gelu_slope(preact):
    return (
        0.5 * (1.0 + lax.erf(preact * 0.7071067811865476))
        + preact * jnp.exp(-0.5 * preact * preact) * 0.3989422804014327
    )


def kernel(
    rows,
    cols,
    x_ref,
    w_ref,
    ct_ref,
    ig_ref,
    wg_ref,
    gat,
    part,
    pin,
    gh,
    full,
    give,
    take,
    pair,
    near_out,
    near_in,
    far_out,
    far_in,
    acc,
    zs,
    zr,
    fs,
    fr,
    ps,
    pr,
    gs,
    gr,
    es,
    er,
    qs,
    qr,
    us,
    ur,
):
    ny = math.isqrt(rows)
    nx = rows // ny
    nz = cols // 2
    r = lax.axis_index("row")
    c = lax.axis_index("col")
    z = c // 2
    core = c % 2
    other = 2 * z + 1 - core
    x0 = r // ny
    y0 = r % ny
    share = x_ref.shape[0]
    width = x_ref.shape[1]
    hidden = w_ref.shape[1]
    toks = ct_ref.shape[0]

    def chip(d):
        return (z + d + 2 * nz) % nz

    def row_at(k):
        return ((x0 + k // ny) % nx) * ny + (y0 + k % ny) % ny

    def row_from(k):
        return ((x0 + nx - k // ny) % nx) * ny + (y0 + ny - k % ny) % ny

    def to(src, dst, send, recv, row, col):
        return pltpu.make_async_remote_copy(
            src_ref=src,
            dst_ref=dst,
            send_sem=send,
            recv_sem=recv,
            device_id=(row, col),
            device_id_type=MESH,
        )

    barrier = pltpu.get_barrier_semaphore()

    for d in (-4, 4, -2, 2, -1, 1):
        pl.semaphore_signal(
            barrier, inc=1, device_id=(r, 2 * chip(d) + core), device_id_type=MESH
        )

    @pl.loop(1, rows)
    def _(k):
        pl.semaphore_signal(barrier, inc=1, device_id=(row_at(k), c), device_id_type=MESH)

    pl.semaphore_signal(barrier, inc=1, device_id=(r, other), device_id_type=MESH)
    pl.semaphore_wait(barrier, 6 + rows - 1 + 1)

    turn = 1 - 2 * core
    messages = [(-4, 0), (4, 0), (-4 * turn, 4 * turn)]
    messages += [(-1, of) for of in (0, 4, -4, 8)] + [(1, of) for of in (0, 4, -4, 8)]
    messages += [(-2, 0), (-2, 4), (2, 0), (2, -4)]

    def gather_send(*numbers):
        for m in numbers:
            hop, of = messages[m]
            slot = 2 * chip(of) + core
            src = x_ref if type(of) is int and of == 0 else gat.at[slot]
            to(src, gat.at[slot], zs.at[m], zr.at[m], r, 2 * chip(hop) + core).start()

    def gather_wait(*numbers):
        for m in numbers:
            hop, of = messages[m]
            slot = 2 * chip(of - hop) + core
            to(x_ref, gat.at[slot], zs.at[m], zr.at[m], r, other).wait_recv()

    def forward(*numbers):
        for m in numbers:
            hop, of = messages[m]
            slot = 2 * chip(of - hop) + core
            to(gat.at[slot], gat.at[slot], fs.at[m], fr.at[m], r, other).start()

    last = len(messages)
    gather_send(0, 1, 3, 7, 11, 13)
    to(x_ref, gat.at[c], fs.at[last], fr.at[last], r, other).start()
    gat[pl.ds(c, 1)] = x_ref[...].reshape(1, share, width)
    gather_wait(3, 7)
    forward(3, 7)
    gather_wait(11, 13)
    forward(11, 13)
    gather_wait(0, 1)
    gather_send(2, 4, 8, 5, 9, 12, 14)
    forward(0, 1)
    gather_wait(4, 5, 8, 9)
    forward(4, 5, 8, 9)
    gather_wait(2)
    gather_send(6, 10)
    forward(2)
    gather_wait(12, 14)
    forward(12, 14)
    gather_wait(6, 10)
    forward(6, 10)

    @pl.loop(0, nz)
    def _(k):
        to(x_ref, gat.at[k], fs.at[k], fr.at[k], r, other).wait_recv()

    for g in range(nx):
        xg = (x0 + g) % nx
        lhs = gat[pl.ds(2 * ny * xg, 2 * ny)].reshape(ny * toks, width)
        block = jnp.dot(lhs, w_ref[...], preferred_element_type=F32)
        if g == 0:
            full[...] = block.reshape(ny, toks, hidden)
            acc[...] = full[pl.ds(y0, 1)].reshape(toks, hidden)
        part[pl.ds(ny * xg, ny)] = block.astype(BF16).reshape(ny, toks, hidden)

        @pl.loop(1 if g == 0 else 0, ny)
        def _(j):
            k = g * ny + j
            peer = row_at(k)
            to(part.at[peer], pin.at[k], ps.at[k], pr.at[k], peer, c).start()

    @pl.loop(1, rows)
    def _(k):
        to(part.at[k], pin.at[k], ps.at[k], pr.at[k], r, other).wait_recv()
        acc[...] += pin[pl.ds(k, 1)].reshape(toks, hidden).astype(F32)

    gh[pl.ds(r, 1)] = (
        (ct_ref[...].astype(F32) * gelu_slope(acc[...])).astype(BF16).reshape(1, toks, hidden)
    )

    @pl.loop(1, rows)
    def _(k):
        to(gh.at[r], gh.at[r], gs.at[k], gr.at[k], row_at(k), c).start()

    for g in range(nx):
        xg = (x0 + nx - g) % nx

        @pl.loop(1 if g == 0 else 0, ny)
        def _(j):
            k = g * ny + j
            to(gh.at[r], gh.at[row_from(k)], gs.at[k], gr.at[k], r, other).wait_recv()

        lhs = gh[pl.ds(ny * xg, ny)].reshape(ny * toks, hidden)
        block = lax.dot_general(
            lhs, w_ref[...], (((1,), (1,)), ((), ())), preferred_element_type=F32
        )
        pair[pl.ds(2 * ny * xg, 2 * ny)] = block.reshape(2 * ny, share, width)
        for j in range(ny):
            at = ny * xg + j
            give[pl.ds(at, 1)] = pair[pl.ds(2 * at + 1 - core, 1)].astype(BF16)
        groups = pl.ds(ny * xg, ny)
        to(give.at[groups], take.at[groups], es.at[g], er.at[g], r, other).start()

    for g in range(nx):
        xg = (x0 + nx - g) % nx
        groups = pl.ds(ny * xg, ny)
        to(give.at[groups], take.at[groups], es.at[g], er.at[g], r, other).wait()

    def chips_term(d):
        at = chip(d)
        return pair[pl.ds(2 * at + core, 1)] + take[pl.ds(at, 1)].astype(F32)

    near = [(-1, 0, (0, 4, -4, 8)), (1, 4, (0, 4, -4, 8)), (-2, 8, (0, -4)), (2, 10, (0, 4))]
    for m, (hop, at, offsets) in enumerate(near):
        for j, of in enumerate(offsets):
            near_out[pl.ds(at + j, 1)] = chips_term(hop + of).astype(BF16)
        span = pl.ds(at, len(offsets))
        to(
            near_out.at[span], near_in.at[span], qs.at[m], qr.at[m], r, 2 * chip(hop) + core
        ).start()
    for m, (hop, at, offsets) in enumerate(near):
        span = pl.ds(at, len(offsets))
        to(near_out.at[span], near_in.at[span], qs.at[m], qr.at[m], r, other).wait_recv()

    def gathered_term(d, *slots):
        term = chips_term(d)
        for slot in slots:
            term = term + near_in[slot : slot + 1].astype(F32)
        return term

    for m, (d, slots) in enumerate(((8, (3, 7)), (4, (1, 5, 11)), (-4, (2, 6, 9)))):
        far_out[m : m + 1] = gathered_term(d, *slots).astype(BF16)
        to(
            far_out.at[m], far_in.at[m], us.at[m], ur.at[m], r, 2 * chip(d) + core
        ).start()

    wg_ref[...] = lax.dot_general(
        gat[...].reshape(rows * toks, width),
        gh[...].reshape(rows * toks, hidden),
        (((0,), (0,)), ((), ())),
        preferred_element_type=F32,
    )

    total = gathered_term(0, 0, 4, 8, 10)
    for m in (1, 2, 0):
        to(far_out.at[m], far_in.at[m], us.at[m], ur.at[m], r, other).wait_recv()
        total = total + far_in[m : m + 1].astype(F32)
    ig_ref[...] = total.reshape(share, width).astype(BF16)

    @pl.loop(0, last)
    def _(k):
        to(x_ref, gat.at[c], zs.at[k], zr.at[k], r, other).wait_send()

    @pl.loop(0, last + 1)
    def _(k):
        to(x_ref, gat.at[c], fs.at[k], fr.at[k], r, other).wait_send()

    for m, (hop, at, offsets) in enumerate(near):
        span = pl.ds(at, len(offsets))
        to(near_out.at[span], near_in.at[span], qs.at[m], qr.at[m], r, other).wait_send()
    for m in range(3):
        to(far_out.at[m], far_in.at[m], us.at[m], ur.at[m], r, other).wait_send()

    @pl.loop(1, rows)
    def _(k):
        to(part.at[k], pin.at[k], ps.at[k], pr.at[k], r, other).wait_send()
        to(gh.at[r], gh.at[r], gs.at[k], gr.at[k], r, other).wait_send()


def shards(rows, cols, inputs, weight, cotangent):
    share, width = inputs.shape
    hidden = weight.shape[1]
    toks = cotangent.shape[0]
    nz = cols // 2
    ny = math.isqrt(rows)
    dma = pltpu.SemaphoreType.DMA
    return pl.pallas_call(
        functools.partial(kernel, rows, cols),
        out_shape=(
            jax.ShapeDtypeStruct((share, width), BF16),
            jax.ShapeDtypeStruct((width, hidden), F32),
        ),
        in_specs=[pl.BlockSpec(memory_space=pltpu.VMEM)] * 3,
        out_specs=(pl.BlockSpec(memory_space=pltpu.VMEM),) * 2,
        scratch_shapes=[
            pltpu.VMEM((cols, share, width), BF16),
            pltpu.VMEM((rows, toks, hidden), BF16),
            pltpu.VMEM((rows, toks, hidden), BF16),
            pltpu.VMEM((rows, toks, hidden), BF16),
            pltpu.VMEM((ny, toks, hidden), F32),
            pltpu.VMEM((nz, share, width), BF16),
            pltpu.VMEM((nz, share, width), BF16),
            pltpu.VMEM((cols, share, width), F32),
            pltpu.VMEM((12, share, width), BF16),
            pltpu.VMEM((12, share, width), BF16),
            pltpu.VMEM((3, share, width), BF16),
            pltpu.VMEM((3, share, width), BF16),
            pltpu.VMEM((toks, hidden), F32),
            dma((nz,)),
            dma((nz,)),
            dma((nz,)),
            dma((nz,)),
            dma((rows,)),
            dma((rows,)),
            dma((rows,)),
            dma((rows,)),
            dma((ny,)),
            dma((ny,)),
            dma((4,)),
            dma((4,)),
            dma((3,)),
            dma((3,)),
        ],
        compiler_params=pltpu.CompilerParams(
            collective_id=0, has_side_effects=True, vmem_limit_bytes=24 * 1024 * 1024
        ),
    )(inputs, weight, cotangent)


def solution(mesh):
    rows, cols = mesh.shape["row"], mesh.shape["col"]
    placed = (P("col", "row"), P("row", "col"), P("row", "col"))
    return jax.shard_map(
        functools.partial(shards, rows, cols),
        mesh=mesh,
        in_specs=placed,
        out_specs=(P("col", "row"), P("row", "col")),
        check_vma=False,
    )
```

```python
import functools
import math

import jax
import jax.numpy as jnp
from jax import lax
from jax.experimental import pallas as pl
from jax.experimental.pallas import tpu as pltpu
from jax.sharding import PartitionSpec as P

MESH = pl.DeviceIdType.MESH
F32 = jnp.float32
BF16 = jnp.bfloat16


def gelu_slope(preact):
    return (
        0.5 * (1.0 + lax.erf(preact * 0.7071067811865476))
        + preact * jnp.exp(-0.5 * preact * preact) * 0.3989422804014327
    )


def kernel(
    rows,
    cols,
    x_ref,
    w_hbm,
    ct_hbm,
    ig_ref,
    wg_ref,
    w_ref,
    ct_ref,
    gat,
    out1,
    in1,
    kept,
    out2,
    in2,
    gh,
    give,
    take,
    pair,
    near_out,
    near_in,
    far_out,
    far_in,
    load,
    zs,
    zr,
    fs,
    fr,
    ss,
    sr,
    gs,
    gr,
    es,
    er,
    qs,
    qr,
    us,
    ur,
):
    n = math.isqrt(rows)
    nz = cols // 2
    r = lax.axis_index("row")
    c = lax.axis_index("col")
    z = c // 2
    core = c % 2
    other = 2 * z + 1 - core
    here = (r // n, r % n)
    share = x_ref.shape[0]
    width = x_ref.shape[1]
    hidden = w_hbm.shape[1]
    half = hidden // 2
    toks = ct_hbm.shape[0]
    sides = (pl.ds(0, half), pl.ds(half, half))

    weight_load = pltpu.make_async_copy(w_hbm, w_ref, load.at[0])
    cotangent_load = pltpu.make_async_copy(ct_hbm, ct_ref, load.at[1])
    own_load = pltpu.make_async_copy(x_ref, gat.at[c], load.at[2])
    weight_load.start()
    cotangent_load.start()
    own_load.start()

    def chip(d):
        return (z + d + 2 * nz) % nz

    def along(axis, d):
        return (here[axis] + n + d) % n

    def row_peer(axis, d):
        if axis == 0:
            return along(0, d) * n + here[1]
        return here[0] * n + along(1, d)

    def to(src, dst, send, recv, row, col):
        return pltpu.make_async_remote_copy(
            src_ref=src,
            dst_ref=dst,
            send_sem=send,
            recv_sem=recv,
            device_id=(row, col),
            device_id_type=MESH,
        )

    barrier = pltpu.get_barrier_semaphore()

    for d in (-4, 4, -2, 2, -1, 1):
        pl.semaphore_signal(
            barrier, inc=1, device_id=(r, 2 * chip(d) + core), device_id_type=MESH
        )

    for axis in (0, 1):
        for d in range(1, n):
            pl.semaphore_signal(
                barrier, inc=1, device_id=(row_peer(axis, d), c), device_id_type=MESH
            )

    pl.semaphore_signal(barrier, inc=1, device_id=(r, other), device_id_type=MESH)
    pl.semaphore_wait(barrier, 6 + 2 * (n - 1) + 1)

    turn = 1 - 2 * core
    messages = [(-4, 0), (4, 0), (-4 * turn, 4 * turn)]
    messages += [(-1, of) for of in (0, 4, -4, 8)] + [(1, of) for of in (0, 4, -4, 8)]
    messages += [(-2, 0), (-2, 4), (2, 0), (2, -4)]

    def gather_send(*numbers):
        for m in numbers:
            hop, of = messages[m]
            slot = 2 * chip(of) + core
            src = x_ref if type(of) is int and of == 0 else gat.at[slot]
            to(src, gat.at[slot], zs.at[m], zr.at[m], r, 2 * chip(hop) + core).start()

    def gather_wait(*numbers):
        for m in numbers:
            hop, of = messages[m]
            slot = 2 * chip(of - hop) + core
            to(x_ref, gat.at[slot], zs.at[m], zr.at[m], r, other).wait_recv()

    def forward(*numbers):
        for m in numbers:
            hop, of = messages[m]
            slot = 2 * chip(of - hop) + core
            to(gat.at[slot], gat.at[slot], fs.at[m], fr.at[m], r, other).start()

    last = len(messages)
    gather_send(0, 1, 3, 7, 11, 13)
    to(x_ref, gat.at[c], fs.at[last], fr.at[last], r, other).start()
    gather_wait(3, 7)
    forward(3, 7)
    gather_wait(11, 13)
    forward(11, 13)
    gather_wait(0, 1)
    gather_send(2, 4, 8, 5, 9, 12, 14)
    forward(0, 1)
    gather_wait(4, 5, 8, 9)
    forward(4, 5, 8, 9)
    gather_wait(2)
    gather_send(6, 10)
    forward(2)
    gather_wait(12, 14)
    forward(12, 14)
    gather_wait(6, 10)
    forward(6, 10)

    @pl.loop(0, nz)
    def _(k):
        to(x_ref, gat.at[k], fs.at[k], fr.at[k], r, other).wait_recv()

    own_load.wait()
    weight_load.wait()

    def tokens_at(axis, at):
        if axis == 0:
            picked = gat[pl.ds(2 * n * at, 2 * n)]
        else:
            picked = jnp.concatenate([gat[pl.ds(2 * (n * v + at), 2)] for v in range(n)], axis=0)
        return picked.reshape(n * toks, width)

    far_first = (2, 1, 3)
    for d in far_first + (0,):
        for h in (0, 1):
            term = jnp.dot(
                tokens_at(h, along(h, d)), w_ref[:, sides[h]], preferred_element_type=F32
            )
            if d == 0:
                kept[h] = term.reshape(n, toks, half)
            else:
                out1[h, d] = term.astype(BF16).reshape(n, toks, half)
                to(
                    out1.at[h, d], in1.at[h, d], ss.at[0, h, d], sr.at[0, h, d], row_peer(h, d), c
                ).start()

    for h in (0, 1):
        for d in (1, 3, 2):
            to(out1.at[h, d], in1.at[h, d], ss.at[0, h, d], sr.at[0, h, d], r, other).wait_recv()
        kept[h] += in1[h, 1].astype(F32) + in1[h, 2].astype(F32) + in1[h, 3].astype(F32)
        for d in far_first:
            at = along(1 - h, d)
            out2[h, d] = kept[h, pl.ds(at, 1)].reshape(toks, half).astype(BF16)
            to(
                out2.at[h, d], in2.at[h, d], ss.at[1, h, d], sr.at[1, h, d], row_peer(1 - h, d), c
            ).start()

    cotangent_load.wait()
    for h in (0, 1):
        preact = kept[h, pl.ds(here[1 - h], 1)].reshape(toks, half)
        for d in (1, 3, 2):
            to(out2.at[h, d], in2.at[h, d], ss.at[1, h, d], sr.at[1, h, d], r, other).wait_recv()
            preact = preact + in2[h, d].astype(F32)
        grad = (ct_ref[:, sides[h]].astype(F32) * gelu_slope(preact)).astype(BF16)
        gh[h, pl.ds(here[1 - h], 1), pl.ds(here[h], 1)] = grad.reshape(1, 1, toks, half)
        own = gh.at[h, here[1 - h], here[h]]
        for d in far_first:
            to(own, own, gs.at[h, 0, d], gr.at[h, 0, d], row_peer(h, d), c).start()
        for d in far_first:
            to(own, own, gs.at[h, 1, d], gr.at[h, 1, d], row_peer(1 - h, d), c).start()

    for e in (1, 3, 2):
        for h in (0, 1):
            block = gh.at[h, here[1 - h], along(h, -e)]
            to(block, block, gs.at[h, 0, e], gr.at[h, 0, e], r, other).wait_recv()
            for d in far_first:
                to(
                    block, block, gs.at[h, 1 + e, d], gr.at[h, 1 + e, d], row_peer(1 - h, d), c
                ).start()

    def second_wait(h, e, d):
        block = gh.at[h, along(1 - h, -d), along(h, -e)]
        to(block, block, gs.at[h, 1 + e, d], gr.at[h, 1 + e, d], r, other).wait_recv()

    for g, e in enumerate((0, 1, 3, 2)):
        xg = along(0, -e)
        for d in (1, 3, 2):
            second_wait(0, e, d)
        if e > 0:
            for f in (0, 1, 3, 2):
                second_wait(1, f, e)
        lhs = jnp.concatenate([gh[0, v, pl.ds(xg, 1)] for v in range(n)], axis=0)
        block = lax.dot_general(
            lhs.reshape(n * toks, half),
            w_ref[:, sides[0]],
            (((1,), (1,)), ((), ())),
            preferred_element_type=F32,
        ) + lax.dot_general(
            gh[1, pl.ds(xg, 1)].reshape(n * toks, half),
            w_ref[:, sides[1]],
            (((1,), (1,)), ((), ())),
            preferred_element_type=F32,
        )
        pair[pl.ds(2 * n * xg, 2 * n)] = block.reshape(2 * n, share, width)
        for j in range(n):
            at = n * xg + j
            give[pl.ds(at, 1)] = pair[pl.ds(2 * at + 1 - core, 1)].astype(BF16)
        groups = pl.ds(n * xg, n)
        to(give.at[groups], take.at[groups], es.at[g], er.at[g], r, other).start()

    for g, e in enumerate((0, 1, 3, 2)):
        groups = pl.ds(n * along(0, -e), n)
        to(give.at[groups], take.at[groups], es.at[g], er.at[g], r, other).wait()

    def chips_term(d):
        at = chip(d)
        return pair[pl.ds(2 * at + core, 1)] + take[pl.ds(at, 1)].astype(F32)

    near = [(-1, 0, (0, 4, -4, 8)), (1, 4, (0, 4, -4, 8)), (-2, 8, (0, -4)), (2, 10, (0, 4))]
    for m, (hop, at, offsets) in enumerate(near):
        for j, of in enumerate(offsets):
            near_out[pl.ds(at + j, 1)] = chips_term(hop + of).astype(BF16)
        span = pl.ds(at, len(offsets))
        to(
            near_out.at[span], near_in.at[span], qs.at[m], qr.at[m], r, 2 * chip(hop) + core
        ).start()
    for m, (hop, at, offsets) in enumerate(near):
        span = pl.ds(at, len(offsets))
        to(near_out.at[span], near_in.at[span], qs.at[m], qr.at[m], r, other).wait_recv()

    def gathered_term(d, *slots):
        term = chips_term(d)
        for slot in slots:
            term = term + near_in[slot : slot + 1].astype(F32)
        return term

    for m, (d, slots) in enumerate(((8, (3, 7)), (4, (1, 5, 11)), (-4, (2, 6, 9)))):
        far_out[m : m + 1] = gathered_term(d, *slots).astype(BF16)
        to(
            far_out.at[m], far_in.at[m], us.at[m], ur.at[m], r, 2 * chip(d) + core
        ).start()

    by_column = jnp.concatenate(
        [gat[2 * (n * u + v) : 2 * (n * u + v) + 2] for v in range(n) for u in range(n)], axis=0
    )
    for h, tokens in ((0, by_column), (1, gat[...])):
        wg_ref[:, sides[h]] = lax.dot_general(
            tokens.reshape(rows * toks, width),
            gh[h].reshape(rows * toks, half),
            (((0,), (0,)), ((), ())),
            preferred_element_type=F32,
        )

    total = gathered_term(0, 0, 4, 8, 10)
    for m in (1, 2, 0):
        to(far_out.at[m], far_in.at[m], us.at[m], ur.at[m], r, other).wait_recv()
        total = total + far_in[m : m + 1].astype(F32)
    ig_ref[...] = total.reshape(share, width).astype(BF16)

    @pl.loop(0, last)
    def _(k):
        to(x_ref, gat.at[c], zs.at[k], zr.at[k], r, other).wait_send()

    @pl.loop(0, last + 1)
    def _(k):
        to(x_ref, gat.at[c], fs.at[k], fr.at[k], r, other).wait_send()

    for m, (hop, at, offsets) in enumerate(near):
        span = pl.ds(at, len(offsets))
        to(near_out.at[span], near_in.at[span], qs.at[m], qr.at[m], r, other).wait_send()
    for m in range(3):
        to(far_out.at[m], far_in.at[m], us.at[m], ur.at[m], r, other).wait_send()

    for h in (0, 1):

        @pl.loop(1, n)
        def _(d):
            to(out1.at[h, d], in1.at[h, d], ss.at[0, h, d], sr.at[0, h, d], r, other).wait_send()
            to(out2.at[h, d], in2.at[h, d], ss.at[1, h, d], sr.at[1, h, d], r, other).wait_send()
            for e in range(n + 1):
                block = gh.at[h, 0, 0]
                to(block, block, gs.at[h, e, d], gr.at[h, e, d], r, other).wait_send()


def shards(rows, cols, inputs, weight, cotangent):
    share, width = inputs.shape
    hidden = weight.shape[1]
    toks = cotangent.shape[0]
    nz = cols // 2
    n = math.isqrt(rows)
    half = hidden // 2
    dma = pltpu.SemaphoreType.DMA
    return pl.pallas_call(
        functools.partial(kernel, rows, cols),
        out_shape=(
            jax.ShapeDtypeStruct((share, width), BF16),
            jax.ShapeDtypeStruct((width, hidden), F32),
        ),
        in_specs=[pl.BlockSpec(memory_space=pltpu.HBM)] * 3,
        out_specs=(pl.BlockSpec(memory_space=pltpu.VMEM),) * 2,
        scratch_shapes=[
            pltpu.VMEM((width, hidden), BF16),
            pltpu.VMEM((toks, hidden), BF16),
            pltpu.VMEM((cols, share, width), BF16),
            pltpu.VMEM((2, n, n, toks, half), BF16),
            pltpu.VMEM((2, n, n, toks, half), BF16),
            pltpu.VMEM((2, n, toks, half), F32),
            pltpu.VMEM((2, n, toks, half), BF16),
            pltpu.VMEM((2, n, toks, half), BF16),
            pltpu.VMEM((2, n, n, toks, half), BF16),
            pltpu.VMEM((nz, share, width), BF16),
            pltpu.VMEM((nz, share, width), BF16),
            pltpu.VMEM((cols, share, width), F32),
            pltpu.VMEM((12, share, width), BF16),
            pltpu.VMEM((12, share, width), BF16),
            pltpu.VMEM((3, share, width), BF16),
            pltpu.VMEM((3, share, width), BF16),
            dma((3,)),
            dma((nz,)),
            dma((nz,)),
            dma((nz,)),
            dma((nz,)),
            dma((2, 2, n)),
            dma((2, 2, n)),
            dma((2, n + 1, n)),
            dma((2, n + 1, n)),
            dma((n,)),
            dma((n,)),
            dma((4,)),
            dma((4,)),
            dma((3,)),
            dma((3,)),
        ],
        compiler_params=pltpu.CompilerParams(
            collective_id=0, has_side_effects=True, vmem_limit_bytes=24 * 1024 * 1024
        ),
    )(inputs, weight, cotangent)


def solution(mesh):
    rows, cols = mesh.shape["row"], mesh.shape["col"]
    placed = (P("col", "row"), P("row", "col"), P("row", "col"))
    return jax.shard_map(
        functools.partial(shards, rows, cols),
        mesh=mesh,
        in_specs=placed,
        out_specs=(P("col", "row"), P("row", "col")),
        check_vma=False,
    )
```

```python
import functools
import math

import jax
import jax.numpy as jnp
from jax import lax
from jax.experimental import pallas as pl
from jax.experimental.pallas import tpu as pltpu
from jax.sharding import PartitionSpec as P

MESH = pl.DeviceIdType.MESH
F32 = jnp.float32
BF16 = jnp.bfloat16


def gelu_slope(preact):
    return (
        0.5 * (1.0 + lax.erf(preact * 0.7071067811865476))
        + preact * jnp.exp(-0.5 * preact * preact) * 0.3989422804014327
    )


def kernel(
    rows,
    cols,
    x_ref,
    w_hbm,
    ct_hbm,
    ig_ref,
    wg_ref,
    w_ref,
    ct_ref,
    gat,
    out1,
    in1,
    kept,
    out2,
    in2,
    gh,
    give,
    take,
    pair,
    near_out,
    near_in,
    far_out,
    far_in,
    load,
    zs,
    zr,
    fs,
    fr,
    ss,
    sr,
    gs,
    gr,
    es,
    er,
    qs,
    qr,
    us,
    ur,
):
    n = math.isqrt(rows)
    nz = cols // 2
    r = lax.axis_index("row")
    c = lax.axis_index("col")
    z = c // 2
    core = c % 2
    other = 2 * z + 1 - core
    here = (r // n, r % n)
    share = x_ref.shape[0]
    width = x_ref.shape[1]
    hidden = w_hbm.shape[1]
    half = hidden // 2
    toks = ct_hbm.shape[0]
    sides = (pl.ds(0, half), pl.ds(half, half))

    weight_load = pltpu.make_async_copy(w_hbm, w_ref, load.at[0])
    cotangent_load = pltpu.make_async_copy(ct_hbm, ct_ref, load.at[1])
    own_load = pltpu.make_async_copy(x_ref, gat.at[c], load.at[2])
    weight_load.start()
    cotangent_load.start()
    own_load.start()

    def chip(d):
        return (z + d + 2 * nz) % nz

    def along(axis, d):
        return (here[axis] + n + d) % n

    def row_peer(axis, d):
        if axis == 0:
            return along(0, d) * n + here[1]
        return here[0] * n + along(1, d)

    def to(src, dst, send, recv, row, col):
        return pltpu.make_async_remote_copy(
            src_ref=src,
            dst_ref=dst,
            send_sem=send,
            recv_sem=recv,
            device_id=(row, col),
            device_id_type=MESH,
        )

    barrier = pltpu.get_barrier_semaphore()

    for d in (-4, 4, -2, 2, -1, 1):
        pl.semaphore_signal(
            barrier, inc=1, device_id=(r, 2 * chip(d) + core), device_id_type=MESH
        )

    for axis in (0, 1):
        for d in range(1, n):
            pl.semaphore_signal(
                barrier, inc=1, device_id=(row_peer(axis, d), c), device_id_type=MESH
            )

    pl.semaphore_signal(barrier, inc=1, device_id=(r, other), device_id_type=MESH)
    pl.semaphore_wait(barrier, 6 + 2 * (n - 1) + 1)

    turn = 1 - 2 * core
    messages = [(-4, 0), (4, 0), (-4 * turn, 4 * turn)]
    messages += [(-1, of) for of in (0, 4, -4, 8)] + [(1, of) for of in (0, 4, -4, 8)]
    messages += [(-2, 0), (-2, 4), (2, 0), (2, -4)]

    def gather_send(*numbers):
        for m in numbers:
            hop, of = messages[m]
            slot = 2 * chip(of) + core
            src = x_ref if type(of) is int and of == 0 else gat.at[slot]
            to(src, gat.at[slot], zs.at[m], zr.at[m], r, 2 * chip(hop) + core).start()

    def gather_wait(*numbers):
        for m in numbers:
            hop, of = messages[m]
            slot = 2 * chip(of - hop) + core
            to(x_ref, gat.at[slot], zs.at[m], zr.at[m], r, other).wait_recv()

    def forward(*numbers):
        for m in numbers:
            hop, of = messages[m]
            slot = 2 * chip(of - hop) + core
            to(gat.at[slot], gat.at[slot], fs.at[m], fr.at[m], r, other).start()

    last = len(messages)
    gather_send(0, 1, 3, 7, 11, 13)
    to(x_ref, gat.at[c], fs.at[last], fr.at[last], r, other).start()
    gather_wait(3, 7)
    forward(3, 7)
    gather_wait(11, 13)
    forward(11, 13)
    gather_wait(0, 1)
    gather_send(2, 4, 8, 5, 9, 12, 14)
    forward(0, 1)
    gather_wait(4, 5, 8, 9)
    forward(4, 5, 8, 9)
    gather_wait(2)
    gather_send(6, 10)
    forward(2)
    gather_wait(12, 14)
    forward(12, 14)
    gather_wait(6, 10)
    forward(6, 10)

    @pl.loop(0, nz)
    def _(k):
        to(x_ref, gat.at[k], fs.at[k], fr.at[k], r, other).wait_recv()

    own_load.wait()
    weight_load.wait()

    def tokens_at(axis, at):
        if axis == 0:
            picked = gat[pl.ds(2 * n * at, 2 * n)]
        else:
            picked = jnp.concatenate([gat[pl.ds(2 * (n * v + at), 2)] for v in range(n)], axis=0)
        return picked.reshape(n * toks, width)

    far_first = (2, 1, 3)
    for d in far_first + (0,):
        for h in (0, 1):
            term = jnp.dot(
                tokens_at(h, along(h, d)), w_ref[:, sides[h]], preferred_element_type=F32
            )
            if d == 0:
                kept[h] = term.reshape(n, toks, half)
            else:
                out1[h, d] = term.astype(BF16).reshape(n, toks, half)
                to(
                    out1.at[h, d], in1.at[h, d], ss.at[0, h, d], sr.at[0, h, d], row_peer(h, d), c
                ).start()

    for h in (0, 1):
        for d in (1, 3, 2):
            to(out1.at[h, d], in1.at[h, d], ss.at[0, h, d], sr.at[0, h, d], r, other).wait_recv()
        kept[h] += in1[h, 1].astype(F32) + in1[h, 2].astype(F32) + in1[h, 3].astype(F32)
        for d in far_first:
            at = along(1 - h, d)
            out2[h, d] = kept[h, pl.ds(at, 1)].reshape(toks, half).astype(BF16)
            to(
                out2.at[h, d], in2.at[h, d], ss.at[1, h, d], sr.at[1, h, d], row_peer(1 - h, d), c
            ).start()

    cotangent_load.wait()
    for h in (0, 1):
        preact = kept[h, pl.ds(here[1 - h], 1)].reshape(toks, half)
        for d in (1, 3, 2):
            to(out2.at[h, d], in2.at[h, d], ss.at[1, h, d], sr.at[1, h, d], r, other).wait_recv()
            preact = preact + in2[h, d].astype(F32)
        grad = (ct_ref[:, sides[h]].astype(F32) * gelu_slope(preact)).astype(BF16)
        gh[h, pl.ds(here[1 - h], 1), pl.ds(here[h], 1)] = grad.reshape(1, 1, toks, half)
        own = gh.at[h, here[1 - h], here[h]]
        for d in far_first:
            to(own, own, gs.at[h, 0, d], gr.at[h, 0, d], row_peer(h, d), c).start()
        for d in (1, 3):
            to(own, own, gs.at[h, 1, d], gr.at[h, 1, d], row_peer(1 - h, d), c).start()

    for e in (1, 3, 2):
        for h in (0, 1):
            block = gh.at[h, here[1 - h], along(h, -e)]
            to(block, block, gs.at[h, 0, e], gr.at[h, 0, e], r, other).wait_recv()
            for d in (1, 3):
                to(
                    block, block, gs.at[h, 1 + e, d], gr.at[h, 1 + e, d], row_peer(1 - h, d), c
                ).start()

    def second_wait(h, e, d):
        block = gh.at[h, along(1 - h, -d), along(h, -e)]
        to(block, block, gs.at[h, 1 + e, d], gr.at[h, 1 + e, d], r, other).wait_recv()

    def pass_on(e):
        for h in (0, 1):
            for d in (1, 3):
                second_wait(h, e, d)
                if (d == 1) == (e < 2):
                    block = gh.at[h, along(1 - h, -d), along(h, -e)]
                    to(
                        block, block, gs.at[h, 1 + e, 2], gr.at[h, 1 + e, 2], row_peer(1 - h, d), c
                    ).start()

    pass_on(0)
    pass_on(1)
    pass_on(3)
    for g, e in enumerate((0, 1, 3, 2)):
        if g == 1:
            pass_on(2)
        xg = along(0, -e)
        second_wait(0, e, 2)
        if e == 2:
            for f in (0, 1, 3, 2):
                second_wait(1, f, 2)
        lhs = jnp.concatenate([gh[0, v, pl.ds(xg, 1)] for v in range(n)], axis=0)
        block = lax.dot_general(
            lhs.reshape(n * toks, half),
            w_ref[:, sides[0]],
            (((1,), (1,)), ((), ())),
            preferred_element_type=F32,
        ) + lax.dot_general(
            gh[1, pl.ds(xg, 1)].reshape(n * toks, half),
            w_ref[:, sides[1]],
            (((1,), (1,)), ((), ())),
            preferred_element_type=F32,
        )
        pair[pl.ds(2 * n * xg, 2 * n)] = block.reshape(2 * n, share, width)
        for j in range(n):
            at = n * xg + j
            give[pl.ds(at, 1)] = pair[pl.ds(2 * at + 1 - core, 1)].astype(BF16)
        groups = pl.ds(n * xg, n)
        to(give.at[groups], take.at[groups], es.at[g], er.at[g], r, other).start()

    for g, e in enumerate((0, 1, 3, 2)):
        groups = pl.ds(n * along(0, -e), n)
        to(give.at[groups], take.at[groups], es.at[g], er.at[g], r, other).wait()

    def chips_term(d):
        at = chip(d)
        return pair[pl.ds(2 * at + core, 1)] + take[pl.ds(at, 1)].astype(F32)

    near = [(-1, 0, (0, 4, -4, 8)), (1, 4, (0, 4, -4, 8)), (-2, 8, (0, -4)), (2, 10, (0, 4))]
    for m, (hop, at, offsets) in enumerate(near):
        for j, of in enumerate(offsets):
            near_out[pl.ds(at + j, 1)] = chips_term(hop + of).astype(BF16)
        span = pl.ds(at, len(offsets))
        to(
            near_out.at[span], near_in.at[span], qs.at[m], qr.at[m], r, 2 * chip(hop) + core
        ).start()
    for m, (hop, at, offsets) in enumerate(near):
        span = pl.ds(at, len(offsets))
        to(near_out.at[span], near_in.at[span], qs.at[m], qr.at[m], r, other).wait_recv()

    def gathered_term(d, *slots):
        term = chips_term(d)
        for slot in slots:
            term = term + near_in[slot : slot + 1].astype(F32)
        return term

    for m, (d, slots) in enumerate(((8, (3, 7)), (4, (1, 5, 11)), (-4, (2, 6, 9)))):
        far_out[m : m + 1] = gathered_term(d, *slots).astype(BF16)
        to(
            far_out.at[m], far_in.at[m], us.at[m], ur.at[m], r, 2 * chip(d) + core
        ).start()

    by_column = jnp.concatenate(
        [gat[2 * (n * u + v) : 2 * (n * u + v) + 2] for v in range(n) for u in range(n)], axis=0
    )
    for h, tokens in ((0, by_column), (1, gat[...])):
        wg_ref[:, sides[h]] = lax.dot_general(
            tokens.reshape(rows * toks, width),
            gh[h].reshape(rows * toks, half),
            (((0,), (0,)), ((), ())),
            preferred_element_type=F32,
        )

    total = gathered_term(0, 0, 4, 8, 10)
    for m in (1, 2, 0):
        to(far_out.at[m], far_in.at[m], us.at[m], ur.at[m], r, other).wait_recv()
        total = total + far_in[m : m + 1].astype(F32)
    ig_ref[...] = total.reshape(share, width).astype(BF16)

    @pl.loop(0, last)
    def _(k):
        to(x_ref, gat.at[c], zs.at[k], zr.at[k], r, other).wait_send()

    @pl.loop(0, last + 1)
    def _(k):
        to(x_ref, gat.at[c], fs.at[k], fr.at[k], r, other).wait_send()

    for m, (hop, at, offsets) in enumerate(near):
        span = pl.ds(at, len(offsets))
        to(near_out.at[span], near_in.at[span], qs.at[m], qr.at[m], r, other).wait_send()
    for m in range(3):
        to(far_out.at[m], far_in.at[m], us.at[m], ur.at[m], r, other).wait_send()

    for h in (0, 1):

        @pl.loop(1, n)
        def _(d):
            to(out1.at[h, d], in1.at[h, d], ss.at[0, h, d], sr.at[0, h, d], r, other).wait_send()
            to(out2.at[h, d], in2.at[h, d], ss.at[1, h, d], sr.at[1, h, d], r, other).wait_send()
            for e in range(n + 1):
                block = gh.at[h, 0, 0]
                to(block, block, gs.at[h, e, d], gr.at[h, e, d], r, other).wait_send()


def shards(rows, cols, inputs, weight, cotangent):
    share, width = inputs.shape
    hidden = weight.shape[1]
    toks = cotangent.shape[0]
    nz = cols // 2
    n = math.isqrt(rows)
    half = hidden // 2
    dma = pltpu.SemaphoreType.DMA
    return pl.pallas_call(
        functools.partial(kernel, rows, cols),
        out_shape=(
            jax.ShapeDtypeStruct((share, width), BF16),
            jax.ShapeDtypeStruct((width, hidden), F32),
        ),
        in_specs=[pl.BlockSpec(memory_space=pltpu.HBM)] * 3,
        out_specs=(pl.BlockSpec(memory_space=pltpu.VMEM),) * 2,
        scratch_shapes=[
            pltpu.VMEM((width, hidden), BF16),
            pltpu.VMEM((toks, hidden), BF16),
            pltpu.VMEM((cols, share, width), BF16),
            pltpu.VMEM((2, n, n, toks, half), BF16),
            pltpu.VMEM((2, n, n, toks, half), BF16),
            pltpu.VMEM((2, n, toks, half), F32),
            pltpu.VMEM((2, n, toks, half), BF16),
            pltpu.VMEM((2, n, toks, half), BF16),
            pltpu.VMEM((2, n, n, toks, half), BF16),
            pltpu.VMEM((nz, share, width), BF16),
            pltpu.VMEM((nz, share, width), BF16),
            pltpu.VMEM((cols, share, width), F32),
            pltpu.VMEM((12, share, width), BF16),
            pltpu.VMEM((12, share, width), BF16),
            pltpu.VMEM((3, share, width), BF16),
            pltpu.VMEM((3, share, width), BF16),
            dma((3,)),
            dma((nz,)),
            dma((nz,)),
            dma((nz,)),
            dma((nz,)),
            dma((2, 2, n)),
            dma((2, 2, n)),
            dma((2, n + 1, n)),
            dma((2, n + 1, n)),
            dma((n,)),
            dma((n,)),
            dma((4,)),
            dma((4,)),
            dma((3,)),
            dma((3,)),
        ],
        compiler_params=pltpu.CompilerParams(
            collective_id=0, has_side_effects=True, vmem_limit_bytes=24 * 1024 * 1024
        ),
    )(*(pltpu.with_memory_space_constraint(a, pltpu.HBM) for a in (inputs, weight, cotangent)))


def solution(mesh):
    rows, cols = mesh.shape["row"], mesh.shape["col"]
    placed = (P("col", "row"), P("row", "col"), P("row", "col"))
    return jax.shard_map(
        functools.partial(shards, rows, cols),
        mesh=mesh,
        in_specs=placed,
        out_specs=(P("col", "row"), P("row", "col")),
        check_vma=False,
    )
```

```python
import functools
import math

import jax
import jax.numpy as jnp
from jax import lax
from jax.experimental import pallas as pl
from jax.experimental.pallas import tpu as pltpu
from jax.sharding import PartitionSpec as P

MESH = pl.DeviceIdType.MESH
F32 = jnp.float32
BF16 = jnp.bfloat16


def gelu_slope(preact):
    return (
        0.5 * (1.0 + lax.erf(preact * 0.7071067811865476))
        + preact * jnp.exp(-0.5 * preact * preact) * 0.3989422804014327
    )


def kernel(
    rows,
    cols,
    x_ref,
    w_hbm,
    ct_hbm,
    ig_ref,
    wg_ref,
    w_ref,
    ct_ref,
    gat,
    out1,
    in1,
    kept,
    out2,
    in2,
    gh,
    give,
    take,
    pair,
    near_out,
    near_in,
    far_out,
    far_in,
    load,
    zs,
    zr,
    fs,
    fr,
    ss,
    sr,
    gs,
    gr,
    es,
    er,
    qs,
    qr,
    us,
    ur,
):
    n = math.isqrt(rows)
    nz = cols // 2
    r = lax.axis_index("row")
    c = lax.axis_index("col")
    z = c // 2
    core = c % 2
    other = 2 * z + 1 - core
    here = (r // n, r % n)
    share = x_ref.shape[0]
    width = x_ref.shape[1]
    hidden = w_hbm.shape[1]
    half = hidden // 2
    toks = ct_hbm.shape[0]
    sides = (pl.ds(0, half), pl.ds(half, half))

    weight_load = pltpu.make_async_copy(w_hbm, w_ref, load.at[0])
    cotangent_load = pltpu.make_async_copy(ct_hbm, ct_ref, load.at[1])
    own_load = pltpu.make_async_copy(x_ref, gat.at[c], load.at[2])
    weight_load.start()
    cotangent_load.start()
    own_load.start()

    def chip(d):
        return (z + d + 2 * nz) % nz

    def along(axis, d):
        return (here[axis] + n + d) % n

    def row_peer(axis, d):
        if axis == 0:
            return along(0, d) * n + here[1]
        return here[0] * n + along(1, d)

    def to(src, dst, send, recv, row, col):
        return pltpu.make_async_remote_copy(
            src_ref=src,
            dst_ref=dst,
            send_sem=send,
            recv_sem=recv,
            device_id=(row, col),
            device_id_type=MESH,
        )

    barrier = pltpu.get_barrier_semaphore()

    for d in (-4, 4, -3, 3, -2, 2, -1, 1):
        pl.semaphore_signal(
            barrier, inc=1, device_id=(r, 2 * chip(d) + core), device_id_type=MESH
        )

    for axis in (0, 1):
        for d in range(1, n):
            pl.semaphore_signal(
                barrier, inc=1, device_id=(row_peer(axis, d), c), device_id_type=MESH
            )

    pl.semaphore_signal(barrier, inc=1, device_id=(r, other), device_id_type=MESH)
    pl.semaphore_wait(barrier, 8 + 2 * (n - 1) + 1)

    turn = 1 - 2 * core
    messages = [(-4, 0), (4, 0), (-4 * turn, 4 * turn)]
    messages += [(-1, 0), (-1, 4), (-1, -4), (-3, 4), (1, 0), (1, 4), (1, -4), (3, -4)]
    messages += [(-2, 0), (-2, 4), (2, 0), (2, -4)]

    def gather_send(*numbers):
        for m in numbers:
            hop, of = messages[m]
            slot = 2 * chip(of) + core
            src = x_ref if type(of) is int and of == 0 else gat.at[slot]
            to(src, gat.at[slot], zs.at[m], zr.at[m], r, 2 * chip(hop) + core).start()

    def gather_wait(*numbers):
        for m in numbers:
            hop, of = messages[m]
            slot = 2 * chip(of - hop) + core
            to(x_ref, gat.at[slot], zs.at[m], zr.at[m], r, other).wait_recv()

    def forward(*numbers):
        for m in numbers:
            hop, of = messages[m]
            slot = 2 * chip(of - hop) + core
            to(gat.at[slot], gat.at[slot], fs.at[m], fr.at[m], r, other).start()

    last = len(messages)
    gather_send(0, 1, 3, 7, 11, 13)
    to(x_ref, gat.at[c], fs.at[last], fr.at[last], r, other).start()
    gather_wait(3, 7)
    forward(3, 7)
    gather_wait(11, 13)
    forward(11, 13)
    gather_wait(0, 1)
    gather_send(2, 6, 10, 4, 8, 5, 9, 12, 14)
    forward(0, 1)
    gather_wait(4, 5, 8, 9)
    forward(4, 5, 8, 9)
    gather_wait(12, 14)
    forward(12, 14)
    gather_wait(6, 10)
    forward(6, 10)
    gather_wait(2)
    forward(2)

    @pl.loop(0, nz)
    def _(k):
        to(x_ref, gat.at[k], fs.at[k], fr.at[k], r, other).wait_recv()

    own_load.wait()
    weight_load.wait()

    def tokens_at(axis, at):
        if axis == 0:
            picked = gat[pl.ds(2 * n * at, 2 * n)]
        else:
            picked = jnp.concatenate([gat[pl.ds(2 * (n * v + at), 2)] for v in range(n)], axis=0)
        return picked.reshape(n * toks, width)

    far_first = (2, 1, 3)
    for d in far_first + (0,):
        for h in (0, 1):
            term = jnp.dot(
                tokens_at(h, along(h, d)), w_ref[:, sides[h]], preferred_element_type=F32
            )
            if d == 0:
                kept[h] = term.reshape(n, toks, half)
            else:
                out1[h, d] = term.astype(BF16).reshape(n, toks, half)
                to(
                    out1.at[h, d], in1.at[h, d], ss.at[0, h, d], sr.at[0, h, d], row_peer(h, d), c
                ).start()

    for h in (0, 1):
        for d in (1, 3, 2):
            to(out1.at[h, d], in1.at[h, d], ss.at[0, h, d], sr.at[0, h, d], r, other).wait_recv()
        kept[h] += in1[h, 1].astype(F32) + in1[h, 2].astype(F32) + in1[h, 3].astype(F32)
        for d in far_first:
            at = along(1 - h, d)
            out2[h, d] = kept[h, pl.ds(at, 1)].reshape(toks, half).astype(BF16)
            to(
                out2.at[h, d], in2.at[h, d], ss.at[1, h, d], sr.at[1, h, d], row_peer(1 - h, d), c
            ).start()

    cotangent_load.wait()
    for h in (0, 1):
        preact = kept[h, pl.ds(here[1 - h], 1)].reshape(toks, half)
        for d in (1, 3, 2):
            to(out2.at[h, d], in2.at[h, d], ss.at[1, h, d], sr.at[1, h, d], r, other).wait_recv()
            preact = preact + in2[h, d].astype(F32)
        grad = (ct_ref[:, sides[h]].astype(F32) * gelu_slope(preact)).astype(BF16)
        gh[h, pl.ds(here[1 - h], 1), pl.ds(here[h], 1)] = grad.reshape(1, 1, toks, half)
        own = gh.at[h, here[1 - h], here[h]]
        for d in far_first:
            to(own, own, gs.at[h, 0, d], gr.at[h, 0, d], row_peer(h, d), c).start()
        for d in (1, 3):
            to(own, own, gs.at[h, 1, d], gr.at[h, 1, d], row_peer(1 - h, d), c).start()

    for e in (1, 3, 2):
        for h in (0, 1):
            block = gh.at[h, here[1 - h], along(h, -e)]
            to(block, block, gs.at[h, 0, e], gr.at[h, 0, e], r, other).wait_recv()
            for d in (1, 3):
                to(
                    block, block, gs.at[h, 1 + e, d], gr.at[h, 1 + e, d], row_peer(1 - h, d), c
                ).start()

    def second_wait(h, e, d):
        block = gh.at[h, along(1 - h, -d), along(h, -e)]
        to(block, block, gs.at[h, 1 + e, d], gr.at[h, 1 + e, d], r, other).wait_recv()

    def pass_on(e):
        for h in (0, 1):
            for d in (1, 3):
                second_wait(h, e, d)
                if (d == 1) == (e < 2):
                    block = gh.at[h, along(1 - h, -d), along(h, -e)]
                    to(
                        block, block, gs.at[h, 1 + e, 2], gr.at[h, 1 + e, 2], row_peer(1 - h, d), c
                    ).start()

    pass_on(0)
    pass_on(1)
    pass_on(3)
    for g, e in enumerate((0, 1, 3, 2)):
        if g == 1:
            pass_on(2)
        xg = along(0, -e)
        second_wait(0, e, 2)
        if e == 2:
            for f in (0, 1, 3, 2):
                second_wait(1, f, 2)
        lhs = jnp.concatenate([gh[0, v, pl.ds(xg, 1)] for v in range(n)], axis=0)
        block = lax.dot_general(
            lhs.reshape(n * toks, half),
            w_ref[:, sides[0]],
            (((1,), (1,)), ((), ())),
            preferred_element_type=F32,
        ) + lax.dot_general(
            gh[1, pl.ds(xg, 1)].reshape(n * toks, half),
            w_ref[:, sides[1]],
            (((1,), (1,)), ((), ())),
            preferred_element_type=F32,
        )
        pair[pl.ds(2 * n * xg, 2 * n)] = block.reshape(2 * n, share, width)
        for j in range(n):
            at = n * xg + j
            give[pl.ds(at, 1)] = pair[pl.ds(2 * at + 1 - core, 1)].astype(BF16)
        groups = pl.ds(n * xg, n)
        to(give.at[groups], take.at[groups], es.at[g], er.at[g], r, other).start()

    for g, e in enumerate((0, 1, 3, 2)):
        groups = pl.ds(n * along(0, -e), n)
        to(give.at[groups], take.at[groups], es.at[g], er.at[g], r, other).wait()

    def chips_term(d):
        at = chip(d)
        return pair[pl.ds(2 * at + core, 1)] + take[pl.ds(at, 1)].astype(F32)

    steps = (1, -1, 2, -2, 3, -3)
    near = [(4 * turn, 8)] + [(d, d + 4 if d > 0 else d - 4) for d in reversed(steps)]
    near += [(d, d) for d in reversed(steps)]

    def near_copy(m, col):
        return to(near_out.at[m], near_in.at[m], qs.at[m], qr.at[m], r, col)

    for m, (hop, keeper) in enumerate(near):
        near_out[m : m + 1] = chips_term(keeper).astype(BF16)
        near_copy(m, 2 * chip(hop) + core).start()
    for m in range(7):
        near_copy(m, other).wait_recv()

    opposite = near_in[0:1].astype(F32)
    for m, d in enumerate((4, -4)):
        term = chips_term(d) + jnp.where(core == m, opposite, 0.0)
        for slot in (2 - m, 4 - m, 6 - m):
            term = term + near_in[slot : slot + 1].astype(F32)
        far_out[m : m + 1] = term.astype(BF16)
        to(
            far_out.at[m], far_in.at[m], us.at[m], ur.at[m], r, 2 * chip(d) + core
        ).start()

    by_column = jnp.concatenate(
        [gat[2 * (n * u + v) : 2 * (n * u + v) + 2] for v in range(n) for u in range(n)], axis=0
    )
    for h, tokens in ((0, by_column), (1, gat[...])):
        wg_ref[:, sides[h]] = lax.dot_general(
            tokens.reshape(rows * toks, width),
            gh[h].reshape(rows * toks, half),
            (((0,), (0,)), ((), ())),
            preferred_element_type=F32,
        )

    total = chips_term(0)
    for m in range(7, 13):
        near_copy(m, other).wait_recv()
        total = total + near_in[m : m + 1].astype(F32)
    for m in range(2):
        to(far_out.at[m], far_in.at[m], us.at[m], ur.at[m], r, other).wait_recv()
        total = total + far_in[m : m + 1].astype(F32)
    ig_ref[...] = total.reshape(share, width).astype(BF16)

    @pl.loop(0, last)
    def _(k):
        to(x_ref, gat.at[c], zs.at[k], zr.at[k], r, other).wait_send()

    @pl.loop(0, last + 1)
    def _(k):
        to(x_ref, gat.at[c], fs.at[k], fr.at[k], r, other).wait_send()

    for m in range(13):
        near_copy(m, other).wait_send()
    for m in range(2):
        to(far_out.at[m], far_in.at[m], us.at[m], ur.at[m], r, other).wait_send()

    for h in (0, 1):

        @pl.loop(1, n)
        def _(d):
            to(out1.at[h, d], in1.at[h, d], ss.at[0, h, d], sr.at[0, h, d], r, other).wait_send()
            to(out2.at[h, d], in2.at[h, d], ss.at[1, h, d], sr.at[1, h, d], r, other).wait_send()
            for e in range(n + 1):
                block = gh.at[h, 0, 0]
                to(block, block, gs.at[h, e, d], gr.at[h, e, d], r, other).wait_send()


def shards(rows, cols, inputs, weight, cotangent):
    share, width = inputs.shape
    hidden = weight.shape[1]
    toks = cotangent.shape[0]
    nz = cols // 2
    n = math.isqrt(rows)
    half = hidden // 2
    dma = pltpu.SemaphoreType.DMA
    return pl.pallas_call(
        functools.partial(kernel, rows, cols),
        out_shape=(
            jax.ShapeDtypeStruct((share, width), BF16),
            jax.ShapeDtypeStruct((width, hidden), F32),
        ),
        in_specs=[pl.BlockSpec(memory_space=pltpu.HBM)] * 3,
        out_specs=(pl.BlockSpec(memory_space=pltpu.VMEM),) * 2,
        scratch_shapes=[
            pltpu.VMEM((width, hidden), BF16),
            pltpu.VMEM((toks, hidden), BF16),
            pltpu.VMEM((cols, share, width), BF16),
            pltpu.VMEM((2, n, n, toks, half), BF16),
            pltpu.VMEM((2, n, n, toks, half), BF16),
            pltpu.VMEM((2, n, toks, half), F32),
            pltpu.VMEM((2, n, toks, half), BF16),
            pltpu.VMEM((2, n, toks, half), BF16),
            pltpu.VMEM((2, n, n, toks, half), BF16),
            pltpu.VMEM((nz, share, width), BF16),
            pltpu.VMEM((nz, share, width), BF16),
            pltpu.VMEM((cols, share, width), F32),
            pltpu.VMEM((13, share, width), BF16),
            pltpu.VMEM((13, share, width), BF16),
            pltpu.VMEM((2, share, width), BF16),
            pltpu.VMEM((2, share, width), BF16),
            dma((3,)),
            dma((nz,)),
            dma((nz,)),
            dma((nz,)),
            dma((nz,)),
            dma((2, 2, n)),
            dma((2, 2, n)),
            dma((2, n + 1, n)),
            dma((2, n + 1, n)),
            dma((n,)),
            dma((n,)),
            dma((13,)),
            dma((13,)),
            dma((2,)),
            dma((2,)),
        ],
        compiler_params=pltpu.CompilerParams(
            collective_id=0, has_side_effects=True, vmem_limit_bytes=24 * 1024 * 1024
        ),
    )(*(pltpu.with_memory_space_constraint(a, pltpu.HBM) for a in (inputs, weight, cotangent)))


def solution(mesh):
    rows, cols = mesh.shape["row"], mesh.shape["col"]
    placed = (P("col", "row"), P("row", "col"), P("row", "col"))
    return jax.shard_map(
        functools.partial(shards, rows, cols),
        mesh=mesh,
        in_specs=placed,
        out_specs=(P("col", "row"), P("row", "col")),
        check_vma=False,
    )
```

```python
import functools
import math

import jax
import jax.numpy as jnp
from jax import lax
from jax.experimental import pallas as pl
from jax.experimental.pallas import tpu as pltpu
from jax.sharding import PartitionSpec as P

MESH = pl.DeviceIdType.MESH
F32 = jnp.float32
BF16 = jnp.bfloat16


def gelu_slope(preact):
    return (
        0.5 * (1.0 + lax.erf(preact * 0.7071067811865476))
        + preact * jnp.exp(-0.5 * preact * preact) * 0.3989422804014327
    )


def kernel(
    rows,
    cols,
    x_ref,
    w_hbm,
    ct_hbm,
    ig_ref,
    wg_ref,
    w_ref,
    ct_ref,
    gat,
    out1,
    in1,
    kept,
    out2,
    in2,
    gh,
    give,
    take,
    pair,
    near_out,
    near_in,
    far_out,
    far_in,
    load,
    zs,
    zr,
    fs,
    fr,
    ss,
    sr,
    gs,
    gr,
    es,
    er,
    qs,
    qr,
    us,
    ur,
):
    n = math.isqrt(rows)
    nz = cols // 2
    r = lax.axis_index("row")
    c = lax.axis_index("col")
    z = c // 2
    core = c % 2
    other = 2 * z + 1 - core
    here = (r // n, r % n)
    share = x_ref.shape[0]
    width = x_ref.shape[1]
    hidden = w_hbm.shape[1]
    half = hidden // 2
    toks = ct_hbm.shape[0]
    sides = (pl.ds(0, half), pl.ds(half, half))

    weight_load = pltpu.make_async_copy(w_hbm, w_ref, load.at[0])
    cotangent_load = pltpu.make_async_copy(ct_hbm, ct_ref, load.at[1])
    own_load = pltpu.make_async_copy(x_ref, gat.at[c], load.at[2])
    weight_load.start()
    cotangent_load.start()
    own_load.start()

    def chip(d):
        return (z + d + 2 * nz) % nz

    def along(axis, d):
        return (here[axis] + n + d) % n

    def row_peer(axis, d):
        if axis == 0:
            return along(0, d) * n + here[1]
        return here[0] * n + along(1, d)

    def to(src, dst, send, recv, row, col):
        return pltpu.make_async_remote_copy(
            src_ref=src,
            dst_ref=dst,
            send_sem=send,
            recv_sem=recv,
            device_id=(row, col),
            device_id_type=MESH,
        )

    barrier = pltpu.get_barrier_semaphore()

    for d in (-4, 4, -3, 3, -2, 2, -1, 1):
        pl.semaphore_signal(
            barrier, inc=1, device_id=(r, 2 * chip(d) + core), device_id_type=MESH
        )

    for axis in (0, 1):
        for d in range(1, n):
            pl.semaphore_signal(
                barrier, inc=1, device_id=(row_peer(axis, d), c), device_id_type=MESH
            )

    pl.semaphore_signal(barrier, inc=1, device_id=(r, other), device_id_type=MESH)
    pl.semaphore_wait(barrier, 8 + 2 * (n - 1) + 1)

    turn = 1 - 2 * core
    messages = [(-4, 0), (4, 0), (-4 * turn, 4 * turn)]
    messages += [(-1, 0), (-1, 4), (-1, -4), (-3, 4), (1, 0), (1, 4), (1, -4), (3, -4)]
    messages += [(-2, 0), (-2, 4), (2, 0), (2, -4)]

    def gather_send(*numbers):
        for m in numbers:
            hop, of = messages[m]
            slot = 2 * chip(of) + core
            src = x_ref if type(of) is int and of == 0 else gat.at[slot]
            to(src, gat.at[slot], zs.at[m], zr.at[m], r, 2 * chip(hop) + core).start()

    def gather_wait(*numbers):
        for m in numbers:
            hop, of = messages[m]
            slot = 2 * chip(of - hop) + core
            to(x_ref, gat.at[slot], zs.at[m], zr.at[m], r, other).wait_recv()

    def forward(*numbers):
        for m in numbers:
            hop, of = messages[m]
            slot = 2 * chip(of - hop) + core
            to(gat.at[slot], gat.at[slot], fs.at[m], fr.at[m], r, other).start()

    last = len(messages)
    gather_send(0, 1, 3, 7, 11, 13)
    to(x_ref, gat.at[c], fs.at[last], fr.at[last], r, other).start()
    gather_wait(3, 7)
    forward(3, 7)
    gather_wait(11, 13)
    forward(11, 13)
    gather_wait(0, 1)
    gather_send(2, 6, 10, 4, 8, 5, 9, 12, 14)
    forward(0, 1)
    gather_wait(4, 5, 8, 9)
    forward(4, 5, 8, 9)
    gather_wait(12, 14)
    forward(12, 14)
    gather_wait(6, 10)
    forward(6, 10)
    gather_wait(2)
    forward(2)

    @pl.loop(0, nz)
    def _(k):
        to(x_ref, gat.at[k], fs.at[k], fr.at[k], r, other).wait_recv()

    own_load.wait()
    weight_load.wait()

    def tokens_at(axis, d):
        at = along(axis, d)
        picked = []
        for off in (1, 2, 3, 0):
            line = along(1 - axis, off)
            block = n * at + line if axis == 0 else n * line + at
            picked.append(gat[pl.ds(2 * block, 2)])
        return jnp.concatenate(picked, axis=0).reshape(n * toks, width)

    def passed(h, d, col):
        span = pl.ds(0, n - 1)
        return to(
            out1.at[h, d, span], in1.at[h, d, span], ss.at[0, h, d], sr.at[0, h, d],
            row_peer(h, d), col,
        )

    def stays(h, d, col):
        return to(
            out1.at[h, d, n - 1], in1.at[h, d, n - 1], ss.at[2, h, d], sr.at[2, h, d],
            row_peer(h, d), col,
        )

    far_first = (2, 1, 3)
    for d in far_first + (0,):
        for h in (0, 1):
            term = jnp.dot(tokens_at(h, d), w_ref[:, sides[h]], preferred_element_type=F32)
            if d == 0:
                kept[h] = term.reshape(n, toks, half)
            else:
                out1[h, d] = term.astype(BF16).reshape(n, toks, half)
                passed(h, d, c).start()
    for d in far_first:
        for h in (0, 1):
            stays(h, d, c).start()

    for h in (0, 1):
        for d in (1, 3, 2):
            passed(h, d, c).wait_recv()
        for d in far_first:
            j = d - 1
            term = kept[h, j] + in1[h, 1, j].astype(F32)
            term = term + in1[h, 2, j].astype(F32) + in1[h, 3, j].astype(F32)
            out2[h, d] = term.astype(BF16)
            to(
                out2.at[h, d], in2.at[h, d], ss.at[1, h, d], sr.at[1, h, d], row_peer(1 - h, d), c
            ).start()

    cotangent_load.wait()
    for h in (0, 1):
        preact = kept[h, n - 1]
        for d in (1, 3, 2):
            stays(h, d, c).wait_recv()
            preact = preact + in1[h, d, n - 1].astype(F32)
        for d in (1, 3, 2):
            to(out2.at[h, d], in2.at[h, d], ss.at[1, h, d], sr.at[1, h, d], r, other).wait_recv()
            preact = preact + in2[h, d].astype(F32)
        grad = (ct_ref[:, sides[h]].astype(F32) * gelu_slope(preact)).astype(BF16)
        gh[h, pl.ds(here[1 - h], 1), pl.ds(here[h], 1)] = grad.reshape(1, 1, toks, half)
        own = gh.at[h, here[1 - h], here[h]]
        for d in far_first:
            to(own, own, gs.at[h, 0, d], gr.at[h, 0, d], row_peer(h, d), c).start()
        for d in (1, 3):
            to(own, own, gs.at[h, 1, d], gr.at[h, 1, d], row_peer(1 - h, d), c).start()

    for e in (1, 3, 2):
        for h in (0, 1):
            block = gh.at[h, here[1 - h], along(h, -e)]
            to(block, block, gs.at[h, 0, e], gr.at[h, 0, e], r, other).wait_recv()
            for d in (1, 3):
                to(
                    block, block, gs.at[h, 1 + e, d], gr.at[h, 1 + e, d], row_peer(1 - h, d), c
                ).start()

    def second_wait(h, e, d):
        block = gh.at[h, along(1 - h, -d), along(h, -e)]
        to(block, block, gs.at[h, 1 + e, d], gr.at[h, 1 + e, d], r, other).wait_recv()

    def pass_on(e):
        for h in (0, 1):
            for d in (1, 3):
                second_wait(h, e, d)
                if (d == 1) == (e < 2):
                    block = gh.at[h, along(1 - h, -d), along(h, -e)]
                    to(
                        block, block, gs.at[h, 1 + e, 2], gr.at[h, 1 + e, 2], row_peer(1 - h, d), c
                    ).start()

    pass_on(0)
    pass_on(1)
    pass_on(3)
    for g, e in enumerate((0, 1, 3, 2)):
        if g == 1:
            pass_on(2)
        xg = along(0, -e)
        second_wait(0, e, 2)
        if e == 2:
            for f in (0, 1, 3, 2):
                second_wait(1, f, 2)
        lhs = jnp.concatenate([gh[0, v, pl.ds(xg, 1)] for v in range(n)], axis=0)
        block = lax.dot_general(
            lhs.reshape(n * toks, half),
            w_ref[:, sides[0]],
            (((1,), (1,)), ((), ())),
            preferred_element_type=F32,
        ) + lax.dot_general(
            gh[1, pl.ds(xg, 1)].reshape(n * toks, half),
            w_ref[:, sides[1]],
            (((1,), (1,)), ((), ())),
            preferred_element_type=F32,
        )
        pair[pl.ds(2 * n * xg, 2 * n)] = block.reshape(2 * n, share, width)
        for j in range(n):
            at = n * xg + j
            give[pl.ds(at, 1)] = pair[pl.ds(2 * at + 1 - core, 1)].astype(BF16)
        groups = pl.ds(n * xg, n)
        to(give.at[groups], take.at[groups], es.at[g], er.at[g], r, other).start()

    for g, e in enumerate((0, 1, 3, 2)):
        groups = pl.ds(n * along(0, -e), n)
        to(give.at[groups], take.at[groups], es.at[g], er.at[g], r, other).wait()

    def chips_term(d):
        at = chip(d)
        return pair[pl.ds(2 * at + core, 1)] + take[pl.ds(at, 1)].astype(F32)

    steps = (1, -1, 2, -2, 3, -3)
    near = [(4 * turn, 8)] + [(d, d + 4 if d > 0 else d - 4) for d in reversed(steps)]
    near += [(d, d) for d in reversed(steps)]

    def near_copy(m, col):
        return to(near_out.at[m], near_in.at[m], qs.at[m], qr.at[m], r, col)

    for m, (hop, keeper) in enumerate(near):
        near_out[m : m + 1] = chips_term(keeper).astype(BF16)
        near_copy(m, 2 * chip(hop) + core).start()
    for m in range(7):
        near_copy(m, other).wait_recv()

    opposite = near_in[0:1].astype(F32)
    for m, d in enumerate((4, -4)):
        term = chips_term(d) + jnp.where(core == m, opposite, 0.0)
        for slot in (2 - m, 4 - m, 6 - m):
            term = term + near_in[slot : slot + 1].astype(F32)
        far_out[m : m + 1] = term.astype(BF16)
        to(
            far_out.at[m], far_in.at[m], us.at[m], ur.at[m], r, 2 * chip(d) + core
        ).start()

    by_column = jnp.concatenate(
        [gat[2 * (n * u + v) : 2 * (n * u + v) + 2] for v in range(n) for u in range(n)], axis=0
    )
    for h, tokens in ((0, by_column), (1, gat[...])):
        wg_ref[:, sides[h]] = lax.dot_general(
            tokens.reshape(rows * toks, width),
            gh[h].reshape(rows * toks, half),
            (((0,), (0,)), ((), ())),
            preferred_element_type=F32,
        )

    total = chips_term(0)
    for m in range(7, 13):
        near_copy(m, other).wait_recv()
        total = total + near_in[m : m + 1].astype(F32)
    for m in range(2):
        to(far_out.at[m], far_in.at[m], us.at[m], ur.at[m], r, other).wait_recv()
        total = total + far_in[m : m + 1].astype(F32)
    ig_ref[...] = total.reshape(share, width).astype(BF16)

    @pl.loop(0, last)
    def _(k):
        to(x_ref, gat.at[c], zs.at[k], zr.at[k], r, other).wait_send()

    @pl.loop(0, last + 1)
    def _(k):
        to(x_ref, gat.at[c], fs.at[k], fr.at[k], r, other).wait_send()

    for m in range(13):
        near_copy(m, other).wait_send()
    for m in range(2):
        to(far_out.at[m], far_in.at[m], us.at[m], ur.at[m], r, other).wait_send()

    for h in (0, 1):

        @pl.loop(1, n)
        def _(d):
            span = pl.ds(0, n - 1)
            to(
                out1.at[h, d, span], in1.at[h, d, span], ss.at[0, h, d], sr.at[0, h, d], r, other
            ).wait_send()
            to(
                out1.at[h, d, 0], in1.at[h, d, 0], ss.at[2, h, d], sr.at[2, h, d], r, other
            ).wait_send()
            to(out2.at[h, d], in2.at[h, d], ss.at[1, h, d], sr.at[1, h, d], r, other).wait_send()
            for e in range(n + 1):
                block = gh.at[h, 0, 0]
                to(block, block, gs.at[h, e, d], gr.at[h, e, d], r, other).wait_send()


def shards(rows, cols, inputs, weight, cotangent):
    share, width = inputs.shape
    hidden = weight.shape[1]
    toks = cotangent.shape[0]
    nz = cols // 2
    n = math.isqrt(rows)
    half = hidden // 2
    dma = pltpu.SemaphoreType.DMA
    return pl.pallas_call(
        functools.partial(kernel, rows, cols),
        out_shape=(
            jax.ShapeDtypeStruct((share, width), BF16),
            jax.ShapeDtypeStruct((width, hidden), F32),
        ),
        in_specs=[pl.BlockSpec(memory_space=pltpu.HBM)] * 3,
        out_specs=(pl.BlockSpec(memory_space=pltpu.VMEM),) * 2,
        scratch_shapes=[
            pltpu.VMEM((width, hidden), BF16),
            pltpu.VMEM((toks, hidden), BF16),
            pltpu.VMEM((cols, share, width), BF16),
            pltpu.VMEM((2, n, n, toks, half), BF16),
            pltpu.VMEM((2, n, n, toks, half), BF16),
            pltpu.VMEM((2, n, toks, half), F32),
            pltpu.VMEM((2, n, toks, half), BF16),
            pltpu.VMEM((2, n, toks, half), BF16),
            pltpu.VMEM((2, n, n, toks, half), BF16),
            pltpu.VMEM((nz, share, width), BF16),
            pltpu.VMEM((nz, share, width), BF16),
            pltpu.VMEM((cols, share, width), F32),
            pltpu.VMEM((13, share, width), BF16),
            pltpu.VMEM((13, share, width), BF16),
            pltpu.VMEM((2, share, width), BF16),
            pltpu.VMEM((2, share, width), BF16),
            dma((3,)),
            dma((nz,)),
            dma((nz,)),
            dma((nz,)),
            dma((nz,)),
            dma((3, 2, n)),
            dma((3, 2, n)),
            dma((2, n + 1, n)),
            dma((2, n + 1, n)),
            dma((n,)),
            dma((n,)),
            dma((13,)),
            dma((13,)),
            dma((2,)),
            dma((2,)),
        ],
        compiler_params=pltpu.CompilerParams(
            collective_id=0, has_side_effects=True, vmem_limit_bytes=24 * 1024 * 1024
        ),
    )(*(pltpu.with_memory_space_constraint(a, pltpu.HBM) for a in (inputs, weight, cotangent)))


def solution(mesh):
    rows, cols = mesh.shape["row"], mesh.shape["col"]
    placed = (P("col", "row"), P("row", "col"), P("row", "col"))
    return jax.shard_map(
        functools.partial(shards, rows, cols),
        mesh=mesh,
        in_specs=placed,
        out_specs=(P("col", "row"), P("row", "col")),
        check_vma=False,
    )
```

```python
import functools
import math

import jax
import jax.numpy as jnp
from jax import lax
from jax.experimental import pallas as pl
from jax.experimental.pallas import tpu as pltpu
from jax.sharding import PartitionSpec as P

MESH = pl.DeviceIdType.MESH
F32 = jnp.float32
BF16 = jnp.bfloat16


def gelu_slope(preact):
    return (
        0.5 * (1.0 + lax.erf(preact * 0.7071067811865476))
        + preact * jnp.exp(-0.5 * preact * preact) * 0.3989422804014327
    )


def kernel(
    rows,
    cols,
    x_ref,
    w_hbm,
    ct_hbm,
    ig_ref,
    wg_ref,
    w_ref,
    ct_ref,
    gat,
    out1,
    in1,
    kept,
    out2,
    in2,
    gh,
    give,
    take,
    pair,
    near_out,
    near_in,
    far_out,
    far_in,
    load,
    zs,
    zr,
    fs,
    fr,
    ss,
    sr,
    gs,
    gr,
    es,
    er,
    qs,
    qr,
    us,
    ur,
):
    n = math.isqrt(rows)
    nz = cols // 2
    r = lax.axis_index("row")
    c = lax.axis_index("col")
    z = c // 2
    core = c % 2
    other = 2 * z + 1 - core
    here = (r // n, r % n)
    share = x_ref.shape[0]
    width = x_ref.shape[1]
    hidden = w_hbm.shape[1]
    half = hidden // 2
    toks = ct_hbm.shape[0]
    sides = (pl.ds(0, half), pl.ds(half, half))

    weight_load = pltpu.make_async_copy(w_hbm, w_ref, load.at[0])
    cotangent_load = pltpu.make_async_copy(ct_hbm, ct_ref, load.at[1])
    own_load = pltpu.make_async_copy(x_ref, gat.at[c], load.at[2])
    weight_load.start()
    cotangent_load.start()
    own_load.start()

    def chip(d):
        return (z + d + 2 * nz) % nz

    def along(axis, d):
        return (here[axis] + n + d) % n

    def row_peer(axis, d):
        if axis == 0:
            return along(0, d) * n + here[1]
        return here[0] * n + along(1, d)

    def to(src, dst, send, recv, row, col):
        return pltpu.make_async_remote_copy(
            src_ref=src,
            dst_ref=dst,
            send_sem=send,
            recv_sem=recv,
            device_id=(row, col),
            device_id_type=MESH,
        )

    barrier = pltpu.get_barrier_semaphore()

    for d in (-4, 4, -3, 3, -2, 2, -1, 1):
        pl.semaphore_signal(
            barrier, inc=1, device_id=(r, 2 * chip(d) + core), device_id_type=MESH
        )

    for axis in (0, 1):
        for d in range(1, n):
            pl.semaphore_signal(
                barrier, inc=1, device_id=(row_peer(axis, d), c), device_id_type=MESH
            )

    pl.semaphore_signal(barrier, inc=1, device_id=(r, other), device_id_type=MESH)
    pl.semaphore_wait(barrier, 8 + 2 * (n - 1) + 1)

    turn = 1 - 2 * core
    messages = [(-4, 0), (4, 0), (-4 * turn, 4 * turn)]
    messages += [(-1, 0), (-1, 4), (-1, -4), (-3, 4), (1, 0), (1, 4), (1, -4), (3, -4)]
    messages += [(-2, 0), (-2, 4), (2, 0), (2, -4)]

    def gather_send(*numbers):
        for m in numbers:
            hop, of = messages[m]
            slot = 2 * chip(of) + core
            src = x_ref if type(of) is int and of == 0 else gat.at[slot]
            to(src, gat.at[slot], zs.at[m], zr.at[m], r, 2 * chip(hop) + core).start()

    def gather_wait(*numbers):
        for m in numbers:
            hop, of = messages[m]
            slot = 2 * chip(of - hop) + core
            to(x_ref, gat.at[slot], zs.at[m], zr.at[m], r, other).wait_recv()

    def forward(*numbers):
        for m in numbers:
            hop, of = messages[m]
            slot = 2 * chip(of - hop) + core
            to(gat.at[slot], gat.at[slot], fs.at[m], fr.at[m], r, other).start()

    last = len(messages)
    gather_send(0, 1, 3, 7, 11, 13)
    to(x_ref, gat.at[c], fs.at[last], fr.at[last], r, other).start()
    gather_wait(3, 7)
    forward(3, 7)
    gather_wait(11, 13)
    forward(11, 13)
    gather_wait(0, 1)
    gather_send(2, 6, 10, 4, 8, 5, 9, 12, 14)
    forward(0, 1)
    gather_wait(4, 5, 8, 9)
    forward(4, 5, 8, 9)
    gather_wait(12, 14)
    forward(12, 14)
    gather_wait(6, 10)
    forward(6, 10)
    gather_wait(2)
    forward(2)

    @pl.loop(0, nz)
    def _(k):
        to(x_ref, gat.at[k], fs.at[k], fr.at[k], r, other).wait_recv()

    own_load.wait()
    weight_load.wait()

    def tokens_at(axis, d):
        at = along(axis, d)
        picked = []
        for off in (1, 2, 3, 0):
            line = along(1 - axis, off)
            block = n * at + line if axis == 0 else n * line + at
            picked.append(gat[pl.ds(2 * block, 2)])
        return jnp.concatenate(picked, axis=0).reshape(n * toks, width)

    def passed(h, d, col):
        span = pl.ds(0, n - 1)
        return to(
            out1.at[h, d, span], in1.at[h, d, span], ss.at[0, h, d], sr.at[0, h, d],
            row_peer(h, d), col,
        )

    def stays(h, d, col):
        return to(
            out1.at[h, d, n - 1], in1.at[h, d, n - 1], ss.at[2, h, d], sr.at[2, h, d],
            row_peer(h, d), col,
        )

    far_first = (2, 1, 3)
    for d in far_first + (0,):
        for h in (0, 1):
            term = jnp.dot(tokens_at(h, d), w_ref[:, sides[h]], preferred_element_type=F32)
            if d == 0:
                kept[h] = term.reshape(n, toks, half)
            else:
                out1[h, d] = term.astype(BF16).reshape(n, toks, half)
                passed(h, d, c).start()
    for d in far_first:
        for h in (0, 1):
            stays(h, d, c).start()

    for h in (0, 1):
        for d in (1, 3, 2):
            passed(h, d, c).wait_recv()
        for d in far_first:
            j = d - 1
            term = kept[h, j] + in1[h, 1, j].astype(F32)
            term = term + in1[h, 2, j].astype(F32) + in1[h, 3, j].astype(F32)
            out2[h, d] = term.astype(BF16)
            to(
                out2.at[h, d], in2.at[h, d], ss.at[1, h, d], sr.at[1, h, d], row_peer(1 - h, d), c
            ).start()

    cotangent_load.wait()
    for h in (0, 1):
        preact = kept[h, n - 1]
        for d in (1, 3, 2):
            stays(h, d, c).wait_recv()
            preact = preact + in1[h, d, n - 1].astype(F32)
        for d in (1, 3, 2):
            to(out2.at[h, d], in2.at[h, d], ss.at[1, h, d], sr.at[1, h, d], r, other).wait_recv()
            preact = preact + in2[h, d].astype(F32)
        grad = (ct_ref[:, sides[h]].astype(F32) * gelu_slope(preact)).astype(BF16)
        gh[h, pl.ds(here[1 - h], 1), pl.ds(here[h], 1)] = grad.reshape(1, 1, toks, half)
        own = gh.at[h, here[1 - h], here[h]]
        for d in far_first:
            to(own, own, gs.at[h, 0, d], gr.at[h, 0, d], row_peer(h, d), c).start()
        for d in (1, 3):
            to(own, own, gs.at[h, 1, d], gr.at[h, 1, d], row_peer(1 - h, d), c).start()

    for e in (1, 3, 2):
        for h in (0, 1):
            block = gh.at[h, here[1 - h], along(h, -e)]
            to(block, block, gs.at[h, 0, e], gr.at[h, 0, e], r, other).wait_recv()
            for d in (1, 3):
                to(
                    block, block, gs.at[h, 1 + e, d], gr.at[h, 1 + e, d], row_peer(1 - h, d), c
                ).start()

    def second_wait(h, e, d):
        block = gh.at[h, along(1 - h, -d), along(h, -e)]
        to(block, block, gs.at[h, 1 + e, d], gr.at[h, 1 + e, d], r, other).wait_recv()

    def pass_on(e):
        for h in (0, 1):
            for d in (1, 3):
                second_wait(h, e, d)
                if (d == 1) == (e < 2):
                    block = gh.at[h, along(1 - h, -d), along(h, -e)]
                    to(
                        block, block, gs.at[h, 1 + e, 2], gr.at[h, 1 + e, 2], row_peer(1 - h, d), c
                    ).start()

    pass_on(0)
    pass_on(1)
    pass_on(3)
    for g, e in enumerate((0, 1, 3, 2)):
        if g == 1:
            pass_on(2)
        xg = along(0, -e)
        second_wait(0, e, 2)
        if e == 2:
            for f in (0, 1, 3, 2):
                second_wait(1, f, 2)
        lhs = jnp.concatenate([gh[0, v, pl.ds(xg, 1)] for v in range(n)], axis=0)
        block = lax.dot_general(
            lhs.reshape(n * toks, half),
            w_ref[:, sides[0]],
            (((1,), (1,)), ((), ())),
            preferred_element_type=F32,
        ) + lax.dot_general(
            gh[1, pl.ds(xg, 1)].reshape(n * toks, half),
            w_ref[:, sides[1]],
            (((1,), (1,)), ((), ())),
            preferred_element_type=F32,
        )
        pair[pl.ds(2 * n * xg, 2 * n)] = block.reshape(2 * n, share, width)
        for j in range(n):
            at = n * xg + j
            give[pl.ds(at, 1)] = pair[pl.ds(2 * at + 1 - core, 1)].astype(BF16)
        groups = pl.ds(n * xg, n)
        to(give.at[groups], take.at[groups], es.at[g], er.at[g], r, other).start()

    for g, e in enumerate((0, 1, 3, 2)):
        groups = pl.ds(n * along(0, -e), n)
        to(give.at[groups], take.at[groups], es.at[g], er.at[g], r, other).wait()

    def chips_term(d):
        at = chip(d)
        return pair[pl.ds(2 * at + core, 1)] + take[pl.ds(at, 1)].astype(F32)

    steps = (1, -1, 2, -2, 3, -3)
    near = [(4 * turn, 8)] + [(d, d + 4 if d > 0 else d - 4) for d in reversed(steps)]
    near += [(d, d) for d in reversed(steps)]

    def near_copy(m, col):
        return to(near_out.at[m], near_in.at[m], qs.at[m], qr.at[m], r, col)

    for m, (hop, keeper) in enumerate(near):
        near_out[m : m + 1] = chips_term(keeper).astype(BF16)
        near_copy(m, 2 * chip(hop) + core).start()

    def weight_half(h, tokens):
        wg_ref[:, sides[h]] = lax.dot_general(
            tokens.reshape(rows * toks, width),
            gh[h].reshape(rows * toks, half),
            (((0,), (0,)), ((), ())),
            preferred_element_type=F32,
        )

    weight_half(1, gat[...])
    for m in range(7):
        near_copy(m, other).wait_recv()

    opposite = near_in[0:1].astype(F32)
    for m, d in enumerate((4, -4)):
        term = chips_term(d) + jnp.where(core == m, opposite, 0.0)
        for slot in (2 - m, 4 - m, 6 - m):
            term = term + near_in[slot : slot + 1].astype(F32)
        far_out[m : m + 1] = term.astype(BF16)
        to(
            far_out.at[m], far_in.at[m], us.at[m], ur.at[m], r, 2 * chip(d) + core
        ).start()

    by_column = jnp.concatenate(
        [gat[2 * (n * u + v) : 2 * (n * u + v) + 2] for v in range(n) for u in range(n)], axis=0
    )
    weight_half(0, by_column)

    total = chips_term(0)
    for m in range(7, 13):
        near_copy(m, other).wait_recv()
        total = total + near_in[m : m + 1].astype(F32)
    for m in range(2):
        to(far_out.at[m], far_in.at[m], us.at[m], ur.at[m], r, other).wait_recv()
        total = total + far_in[m : m + 1].astype(F32)
    ig_ref[...] = total.reshape(share, width).astype(BF16)

    @pl.loop(0, last)
    def _(k):
        to(x_ref, gat.at[c], zs.at[k], zr.at[k], r, other).wait_send()

    @pl.loop(0, last + 1)
    def _(k):
        to(x_ref, gat.at[c], fs.at[k], fr.at[k], r, other).wait_send()

    for m in range(13):
        near_copy(m, other).wait_send()
    for m in range(2):
        to(far_out.at[m], far_in.at[m], us.at[m], ur.at[m], r, other).wait_send()

    for h in (0, 1):

        @pl.loop(1, n)
        def _(d):
            span = pl.ds(0, n - 1)
            to(
                out1.at[h, d, span], in1.at[h, d, span], ss.at[0, h, d], sr.at[0, h, d], r, other
            ).wait_send()
            to(
                out1.at[h, d, 0], in1.at[h, d, 0], ss.at[2, h, d], sr.at[2, h, d], r, other
            ).wait_send()
            to(out2.at[h, d], in2.at[h, d], ss.at[1, h, d], sr.at[1, h, d], r, other).wait_send()
            for e in range(n + 1):
                block = gh.at[h, 0, 0]
                to(block, block, gs.at[h, e, d], gr.at[h, e, d], r, other).wait_send()


def shards(rows, cols, inputs, weight, cotangent):
    share, width = inputs.shape
    hidden = weight.shape[1]
    toks = cotangent.shape[0]
    nz = cols // 2
    n = math.isqrt(rows)
    half = hidden // 2
    dma = pltpu.SemaphoreType.DMA
    return pl.pallas_call(
        functools.partial(kernel, rows, cols),
        out_shape=(
            jax.ShapeDtypeStruct((share, width), BF16),
            jax.ShapeDtypeStruct((width, hidden), F32),
        ),
        in_specs=[pl.BlockSpec(memory_space=pltpu.HBM)] * 3,
        out_specs=(pl.BlockSpec(memory_space=pltpu.VMEM),) * 2,
        scratch_shapes=[
            pltpu.VMEM((width, hidden), BF16),
            pltpu.VMEM((toks, hidden), BF16),
            pltpu.VMEM((cols, share, width), BF16),
            pltpu.VMEM((2, n, n, toks, half), BF16),
            pltpu.VMEM((2, n, n, toks, half), BF16),
            pltpu.VMEM((2, n, toks, half), F32),
            pltpu.VMEM((2, n, toks, half), BF16),
            pltpu.VMEM((2, n, toks, half), BF16),
            pltpu.VMEM((2, n, n, toks, half), BF16),
            pltpu.VMEM((nz, share, width), BF16),
            pltpu.VMEM((nz, share, width), BF16),
            pltpu.VMEM((cols, share, width), F32),
            pltpu.VMEM((13, share, width), BF16),
            pltpu.VMEM((13, share, width), BF16),
            pltpu.VMEM((2, share, width), BF16),
            pltpu.VMEM((2, share, width), BF16),
            dma((3,)),
            dma((nz,)),
            dma((nz,)),
            dma((nz,)),
            dma((nz,)),
            dma((3, 2, n)),
            dma((3, 2, n)),
            dma((2, n + 1, n)),
            dma((2, n + 1, n)),
            dma((n,)),
            dma((n,)),
            dma((13,)),
            dma((13,)),
            dma((2,)),
            dma((2,)),
        ],
        compiler_params=pltpu.CompilerParams(
            collective_id=0, has_side_effects=True, vmem_limit_bytes=24 * 1024 * 1024
        ),
    )(*(pltpu.with_memory_space_constraint(a, pltpu.HBM) for a in (inputs, weight, cotangent)))


def solution(mesh):
    rows, cols = mesh.shape["row"], mesh.shape["col"]
    placed = (P("col", "row"), P("row", "col"), P("row", "col"))
    return jax.shard_map(
        functools.partial(shards, rows, cols),
        mesh=mesh,
        in_specs=placed,
        out_specs=(P("col", "row"), P("row", "col")),
        check_vma=False,
    )
```
